512 devices in a mesh: comp: 16 (over z_lo, core), feat: 32 (over x, y, z_hi).
Axes of the slice: x: 4, y: 4, z: 16 (z_hi: 2, z_lo: 8; z = z_hi * 8 + z_lo), core: 2. Of those that a mesh axis runs over, the one named last changes fastest.
Arguments:
- samples: float32 [1, 192, 28672], P(None, None, 'feat'), may hold values from -20 to 20, as said below
- start_vectors: float32 [1024, 28672], P('comp', 'feat'), may hold values from -8 to 8
Outputs:
- vectors: float32 [1024, 28672], P('comp', 'feat')
The draws below stay inside these ranges and needn't reach their ends.
Inputs may be any that keep to these rules, and one draw needn't show every extreme that they name: `samples`: activation rows with feature scales that differ over a factor of ten.
All inputs are finite; a program needn't handle non-finite values.
Results may differ from the reference program's by a relative error of at most 0.0001.
Values sent between devices are 32-bit elements; how exact they have to be, the bound alone decides.
A program may use at most 64 MiB of HBM per device.

```python
import math
import jax
import jax.numpy as jnp
from jax import lax

D = 28672
ROWS = 192
STEPS = 1
COMPONENTS = 1024


def draw_samples(key, part):
    key_base, key_rough = jax.random.split(jax.random.fold_in(key, 11), 2)
    position = jnp.arange(D, dtype=jnp.float32) / D
    rough = jax.random.uniform(key_rough, (D,), jnp.float32, 0.6, 1.4)
    scales = 10.0 ** (position - 0.5) * rough
    values = jax.random.normal(key_base, (STEPS, ROWS, D), jnp.float32) * scales
    return jnp.clip(values, -20.0, 20.0)


def draw_start_vectors(key, part):
    key_base, key_rough = jax.random.split(jax.random.fold_in(key, 23), 2)
    position = jnp.arange(D, dtype=jnp.float32) / D
    rough = jax.random.uniform(key_rough, (D,), jnp.float32, 0.5, 1.5)
    values = jax.random.normal(key_base, (COMPONENTS, D), jnp.float32) * 3.0 ** (2.0 * position - 1.0) * rough
    return jnp.clip(values, -8.0, 8.0)


def setup_inputs(seed: int = 0) -> dict:
    streams_of = jax.random.split(jax.random.key(seed), 3)
    return {
        "samples": draw_samples(jax.random.fold_in(streams_of[2], 71), 0),
        "start_vectors": draw_start_vectors(jax.random.fold_in(streams_of[2], 71), 0),
    }


step_rate = 0.1
epsilon = 1e-06
highest = lax.Precision.HIGHEST

def normalize(updated):
    return updated * lax.rsqrt(lax.optimization_barrier(jnp.mean(updated * updated, axis=1, keepdims=True)) + epsilon)

def reference(samples, start_vectors):
    root_width = math.sqrt(D)
    earlier = jnp.arange(COMPONENTS, dtype=jnp.int32)[:, None] < jnp.arange(COMPONENTS, dtype=jnp.int32)[None, :]
    vector = normalize(start_vectors)
    for turn_index in range(STEPS):
        sample = samples[turn_index]
        images = jnp.einsum('rd,kd->rk', sample, vector, precision=highest) / root_width
        intersection = jnp.einsum('rj,ri->ji', images, images, precision=highest) / ROWS
        coupling = jnp.where(earlier, intersection, jnp.float32(0.0))
        penalty = jnp.einsum('ji,jd->id', coupling, vector, precision=highest)
        gradient = root_width * jnp.einsum('rk,rd->kd', images, sample, precision=highest) / ROWS - penalty
        vector = normalize(vector + step_rate * gradient)
    return vector
```

```python
import functools
import math

import jax
import jax.numpy as jnp
from jax import lax
from jax.experimental import pallas as pl
from jax.experimental.pallas import tpu as pltpu
from jax.sharding import PartitionSpec as P

MESH = pl.DeviceIdType.MESH
step_rate = 0.1
epsilon = 1e-06
highest = lax.Precision.HIGHEST

GEOMETRY = dict(planes=16, highs=2, lows=8)
SUB = 24


def dot(a, b, ca, cb):
    return lax.dot_general(
        a, b, (((ca,), (cb,)), ((), ())), precision=highest, preferred_element_type=jnp.float32
    )


def landed(ref, sem):
    pltpu.make_async_copy(ref, ref, sem).wait()


def kernel(
    planes, highs, lows, sub, features,
    s_hbm, u_hbm, out_ref,
    s_v, u_pad, u_chip, p_v, rs_v, zs_v, zr_v, tot_v, x_v, v_v, xt_v, ct_v, own_v, in_v, o_v, new_v, fin_v,
    ld_sem, ux_send, ux_recv, rs_send, rs_recv, z_send, z_recv, ag_send, ag_recv,
    ch_send, ch_recv, rl_send, rl_recv, fin_send, fin_recv,
):
    rows, width = s_v.shape
    half = rows // 2
    tiles = half // 8 + 1
    group = 64
    blocks = width // 128
    subs = half // sub
    feats = planes * highs
    root = math.sqrt(features)

    comp = lax.axis_index("comp")
    feat = lax.axis_index("feat")
    core = lax.rem(comp, 2)
    low = lax.div(comp, 2)
    high = lax.rem(feat, highs)
    plane = lax.div(feat, highs)
    partner = (low * 2 + 1 - core, feat)
    first = low == 0
    last = low == lows - 1
    mine = plane < tiles
    my_rows = pl.multiple_of(core * half, 8)

    load_s = pltpu.make_async_copy(s_hbm.at[0], s_v, ld_sem.at[0])
    load_u = pltpu.make_async_copy(u_hbm, u_pad.at[pl.ds(group, group)], ld_sem.at[1])
    own_group = pl.ds(pl.multiple_of(core * group, 8), group)
    load_c = pltpu.make_async_copy(u_hbm, u_chip.at[own_group], ld_sem.at[2])
    load_u.start()
    load_s.start()
    load_c.start()

    barrier = pltpu.get_barrier_semaphore()

    def plane_peer(d):
        q = lax.rem(plane * 2 + core + d, 2 * planes)
        p = lax.div(q, 2)
        return low * 2 + lax.rem(q, 2), p * highs + high

    def greet(d, carry):
        pl.semaphore_signal(barrier, inc=1, device_id=plane_peer(d), device_id_type=MESH)
        return carry

    across = (comp, plane * highs + 1 - high)
    right = (comp + 2, feat)
    left = (comp - 2, feat)
    pl.semaphore_signal(barrier, inc=1, device_id=across, device_id_type=MESH)
    lax.fori_loop(1, 2 * planes, greet, 0)

    @pl.when(jnp.logical_not(first))
    def _():
        pl.semaphore_signal(barrier, inc=1, device_id=left, device_id_type=MESH)

    @pl.when(jnp.logical_not(last))
    def _():
        pl.semaphore_signal(barrier, inc=1, device_id=right, device_id_type=MESH)

    u_pad[0:group, :] = jnp.zeros((group, width), jnp.float32)
    u_pad[2 * group : 3 * group, :] = jnp.zeros((group, width), jnp.float32)
    load_u.wait()
    u_own = u_pad[group : 2 * group, :]
    squares = jnp.zeros((group, 128), jnp.float32)
    for b in range(blocks):
        piece = u_own[:, b * 128 : (b + 1) * 128]
        squares = squares + piece * piece
    squares = jnp.concatenate([squares, squares], axis=0)
    p_v[tiles - 1] = dot(jnp.ones((8, 128), jnp.float32), squares, 1, 1)
    load_s.wait()
    projected = dot(s_v[0:half, :], u_pad[group : 3 * group, :], 1, 1) + dot(
        s_v[half:rows, :], u_pad[0 : 2 * group, :], 1, 1
    )
    for t in range(tiles - 1):
        p_v[t] = projected[8 * t : 8 * t + 8, :]

    pl.semaphore_wait(
        barrier,
        2 * planes
        + jnp.where(first, 0, 1).astype(jnp.int32)
        + jnp.where(last, 0, 1).astype(jnp.int32),
    )

    def scatter(t, wait):
        copy = pltpu.make_async_remote_copy(
            src_ref=p_v.at[t],
            dst_ref=rs_v.at[plane],
            send_sem=rs_send.at[t],
            recv_sem=rs_recv.at[plane],
            device_id=(comp, t * highs + high),
            device_id_type=MESH,
        )

        @pl.when(t != plane)
        def _():
            if wait:
                copy.wait_send()
            else:
                copy.start()

    def scatter_start(t, carry):
        scatter(t, False)
        return carry

    lax.fori_loop(0, tiles, scatter_start, 0)

    load_c.wait()
    to_partner = pltpu.make_async_remote_copy(
        src_ref=u_chip.at[own_group],
        dst_ref=u_chip.at[own_group],
        send_sem=ux_send,
        recv_sem=ux_recv,
        device_id=partner,
        device_id_type=MESH,
    )
    to_partner.start()

    exchange = pltpu.make_async_remote_copy(
        src_ref=zs_v, dst_ref=zr_v, send_sem=z_send, recv_sem=z_recv, device_id=across, device_id_type=MESH
    )

    def spread(d):
        return pltpu.make_async_remote_copy(
            src_ref=tot_v,
            dst_ref=x_v.at[core, plane],
            send_sem=ag_send.at[d],
            recv_sem=ag_recv.at[core, plane],
            device_id=plane_peer(d),
            device_id_type=MESH,
        )

    @pl.when(mine)
    def _():
        rs_v[plane] = p_v[plane]

        def arrive(p, carry):
            @pl.when(p != plane)
            def _():
                landed(rs_v.at[p], rs_recv.at[p])

            return carry

        lax.fori_loop(0, planes, arrive, 0)
        total = rs_v[0]
        for p in range(1, planes):
            total = total + rs_v[p]
        zs_v[...] = total
        exchange.start()
        exchange.wait_recv()
        total = zs_v[...] + zr_v[...]
        tot_v[...] = total

        def spread_start(d, carry):
            spread(d).start()
            return carry

        lax.fori_loop(1, 2 * planes, spread_start, 0)
        x_v[core, plane] = total

    landed(u_chip.at[pl.ds(pl.multiple_of((1 - core) * group, 8), group)], ux_recv)
    to_partner.wait_send()

    def gathered(i, carry):
        g = lax.div(i, tiles)
        t = lax.rem(i, tiles)

        @pl.when(jnp.logical_or(g != core, t != plane))
        def _():
            landed(x_v.at[g, t], ag_recv.at[g, t])

        return carry

    lax.fori_loop(0, 2 * tiles, gathered, 0)

    lane = lax.broadcasted_iota(jnp.int32, (8, 128), 1)
    scale0 = lax.rsqrt(x_v[0, tiles - 1] / features + epsilon)
    scale1 = lax.rsqrt(x_v[1, tiles - 1] / features + epsilon)
    scale_row = jnp.where(lane < group, scale0, scale1)
    for t in range(tiles - 1):
        x0 = x_v[0, t] * scale0 / root
        x1 = x_v[1, t] * scale1 / root
        a = jnp.where(lane < group, x0, pltpu.roll(x1, 64, 1))
        b = jnp.where(lane < group, pltpu.roll(x0, 64, 1), x1)
        rs_rows = pl.ds(8 * t, 8)
        xc_rows = pl.ds(half + 8 * t, 8)
        xt_v[rs_rows, :] = a
        xt_v[xc_rows, :] = b
    eye = lax.broadcasted_iota(jnp.int32, (128, 128), 0) == lax.broadcasted_iota(jnp.int32, (128, 128), 1)
    scale_col = jnp.sum(
        jnp.where(eye, jnp.broadcast_to(scale_row[0:1, :], (128, 128)), 0.0), axis=1, keepdims=True
    )
    v_v[...] = u_chip[...] * scale_col
    x_half = xt_v[pl.ds(my_rows, half), :]
    for b in range(blocks):
        own_v[b] = dot(x_half, v_v[:, b * 128 : (b + 1) * 128], 1, 0)

    def base():
        x_chip = xt_v[...]
        pairs = dot(x_chip, x_chip, 0, 0) / rows
        i = lax.broadcasted_iota(jnp.int32, (128, 128), 0)
        j = lax.broadcasted_iota(jnp.int32, (128, 128), 1)
        ct_v[...] = jnp.where(j < i, pairs, 0.0)
        pull = dot(x_chip, s_v[...], 0, 0) * (root / rows) - dot(ct_v[...], v_v[...], 1, 0)
        u_chip[...] = v_v[...] + step_rate * pull
        new_v[...] = u_chip[own_group, :]

    early = low >= lows // 2 - 1

    @pl.when(early)
    def _():
        base()

    def hop(b, s):
        i = b * subs + s
        here = pl.ds(pl.multiple_of(my_rows + s * sub, 8), sub)
        there = pl.ds(pl.multiple_of(s * sub, 8), sub)
        forward = pltpu.make_async_remote_copy(
            src_ref=o_v.at[b, there],
            dst_ref=in_v.at[b, here],
            send_sem=ch_send.at[i],
            recv_sem=ch_recv.at[i],
            device_id=right,
            device_id_type=MESH,
        )
        relay = pltpu.make_async_remote_copy(
            src_ref=in_v.at[b, here],
            dst_ref=in_v.at[b, here],
            send_sem=rl_send.at[i],
            recv_sem=rl_recv.at[i],
            device_id=partner,
            device_id_type=MESH,
        )
        return here, there, forward, relay

    def finish(b):
        def arrived(s, carry):
            other = pl.ds(pl.multiple_of((1 - core) * half + s * sub, 8), sub)
            landed(in_v.at[b, other], rl_recv.at[b * subs + s])
            return carry

        lax.fori_loop(0, subs, arrived, 0)
        pull = dot(xt_v[...], in_v[b], 0, 0) * (step_rate / rows)
        ct_v[...] = pull
        columns = pl.ds(pl.multiple_of(b * 128, 128), 128)
        new_v[:, columns] = new_v[:, columns] - ct_v[own_group, :]

    def chain(b, carry):
        def one(s, carry):
            here, there, forward, relay = hop(b, s)

            @pl.when(first)
            def _():
                o_v[b, there] = own_v[b, there]
                forward.start()

            @pl.when(jnp.logical_not(first))
            def _():
                landed(in_v.at[b, here], ch_recv.at[b * subs + s])

                @pl.when(jnp.logical_not(last))
                def _():
                    o_v[b, there] = in_v[b, here] + own_v[b, there]
                    forward.start()

                relay.start()

            return carry

        lax.fori_loop(0, subs, one, 0)

        @pl.when(jnp.logical_and(last, b > 0))
        def _():
            finish(b - 1)

        return carry

    lax.fori_loop(0, blocks, chain, 0)

    @pl.when(last)
    def _():
        finish(blocks - 1)

    @pl.when(jnp.logical_not(early))
    def _():
        base()

    @pl.when(jnp.logical_not(jnp.logical_or(first, last)))
    def _():
        def finish_all(b, carry):
            finish(b)
            return carry

        lax.fori_loop(0, blocks, finish_all, 0)

    squares = jnp.zeros((group, 128), jnp.float32)
    for b in range(blocks):
        piece = new_v[:, b * 128 : (b + 1) * 128]
        squares = squares + piece * piece
    column = jnp.sum(squares, axis=1, keepdims=True)
    eye_half = lax.broadcasted_iota(jnp.int32, (group, 128), 0) == lax.broadcasted_iota(
        jnp.int32, (group, 128), 1
    )
    fin_v[feat] = jnp.sum(jnp.where(eye_half, column, 0.0), axis=0, keepdims=True)

    def tell(d):
        q = lax.rem(feat + d, feats)
        return pltpu.make_async_remote_copy(
            src_ref=fin_v.at[feat],
            dst_ref=fin_v.at[feat],
            send_sem=fin_send.at[d],
            recv_sem=fin_recv.at[feat],
            device_id=(comp, q),
            device_id_type=MESH,
        )

    def tell_start(d, carry):
        tell(d).start()
        return carry

    lax.fori_loop(1, feats, tell_start, 0)

    def told(d, carry):
        q = lax.rem(feat + d, feats)
        landed(fin_v.at[q], fin_recv.at[q])
        return carry

    lax.fori_loop(1, feats, told, 0)
    total = fin_v[0]
    for q in range(1, feats):
        total = total + fin_v[q]
    scale = lax.rsqrt(
        jnp.sum(jnp.where(eye_half, jnp.broadcast_to(total, (group, 128)), 0.0), axis=1, keepdims=True)
        / features
        + epsilon
    )
    out_ref[...] = new_v[...] * scale

    def scatter_end(t, carry):
        scatter(t, True)
        return carry

    lax.fori_loop(0, tiles, scatter_end, 0)

    @pl.when(mine)
    def _():
        exchange.wait_send()

        def spread_end(d, carry):
            spread(d).wait_send()
            return carry

        lax.fori_loop(1, 2 * planes, spread_end, 0)

    def chain_end(i, carry):
        here, there, forward, relay = hop(lax.div(i, subs), lax.rem(i, subs))

        @pl.when(jnp.logical_not(last))
        def _():
            forward.wait_send()

        @pl.when(jnp.logical_not(first))
        def _():
            relay.wait_send()

        return carry

    lax.fori_loop(0, blocks * subs, chain_end, 0)

    def tell_end(d, carry):
        tell(d).wait_send()
        return carry

    lax.fori_loop(1, feats, tell_end, 0)


def step(planes, highs, lows, sub, samples, start_vectors):
    _, rows, width = samples.shape
    group = start_vectors.shape[0]
    feats = planes * highs
    half = rows // 2
    tiles = half // 8 + 1
    blocks = width // 128
    chunks = blocks * (half // sub)
    dma = pltpu.SemaphoreType.DMA
    f32 = jnp.float32
    return pl.pallas_call(
        functools.partial(kernel, planes, highs, lows, sub, width * feats),
        out_shape=jax.ShapeDtypeStruct((group, width), f32),
        in_specs=[pl.BlockSpec(memory_space=pl.ANY)] * 2,
        out_specs=pl.BlockSpec(memory_space=pltpu.VMEM),
        scratch_shapes=[
            pltpu.VMEM((rows, width), f32),
            pltpu.VMEM((3 * group, width), f32),
            pltpu.VMEM((2 * group, width), f32),
            pltpu.VMEM((tiles, 8, 128), f32),
            pltpu.VMEM((planes, 8, 128), f32),
            pltpu.VMEM((8, 128), f32),
            pltpu.VMEM((8, 128), f32),
            pltpu.VMEM((8, 128), f32),
            pltpu.VMEM((2, tiles, 8, 128), f32),
            pltpu.VMEM((2 * group, width), f32),
            pltpu.VMEM((rows, 128), f32),
            pltpu.VMEM((128, 128), f32),
            pltpu.VMEM((blocks, half, 128), f32),
            pltpu.VMEM((blocks, rows, 128), f32),
            pltpu.VMEM((blocks, half, 128), f32),
            pltpu.VMEM((group, width), f32),
            pltpu.VMEM((feats, 1, 128), f32),
            dma((3,)),
            dma,
            dma,
            dma((tiles,)),
            dma((planes,)),
            dma,
            dma,
            dma((2 * planes,)),
            dma((2, tiles)),
            dma((chunks,)),
            dma((chunks,)),
            dma((chunks,)),
            dma((chunks,)),
            dma((feats,)),
            dma((feats,)),
        ],
        compiler_params=pltpu.CompilerParams(collective_id=0, has_side_effects=True),
    )(samples, start_vectors)


def solution(mesh, sub=SUB, planes=16, highs=2, lows=8):
    in_specs = (P(None, None, "feat"), P("comp", "feat"))
    return jax.shard_map(
        functools.partial(step, planes, highs, lows, sub),
        mesh=mesh,
        in_specs=in_specs,
        out_specs=P("comp", "feat"),
        check_vma=False,
    )
```

```python
import functools
import math

import jax
import jax.numpy as jnp
from jax import lax
from jax.experimental import pallas as pl
from jax.experimental.pallas import tpu as pltpu
from jax.sharding import PartitionSpec as P

MESH = pl.DeviceIdType.MESH
step_rate = 0.1
epsilon = 1e-06
highest = lax.Precision.HIGHEST

GEOMETRY = dict(planes=16, highs=2, lows=8)
SUB = 24


def dot(a, b, ca, cb):
    return lax.dot_general(
        a, b, (((ca,), (cb,)), ((), ())), precision=highest, preferred_element_type=jnp.float32
    )


def landed(ref, sem):
    pltpu.make_async_copy(ref, ref, sem).wait()


def kernel(
    planes, highs, lows, sub, features,
    s_hbm, u_hbm, out_hbm, scale_ref,
    new_v, s_v, u_pad, u_set, p_v, rs_v, zs_v, zr_v, tot_v, x_v, v_v, xt_v, xtt_v, own_v, in_v, o_v, fin_v,
    ld_sem, ux_send, ux_recv, rs_send, rs_recv, z_send, z_recv, ag_send, ag_recv,
    ch_send, lf_send, ch_recv, rl_send, rl_recv, fin_send, fin_recv, ready,
):
    rows, width = s_v.shape
    half = rows // 2
    tiles = half // 8 + 1
    group = 64
    blocks = width // 128
    subs = half // sub
    feats = planes * highs
    root = math.sqrt(features)

    comp = lax.axis_index("comp")
    feat = lax.axis_index("feat")
    core = lax.rem(comp, 2)
    low = lax.div(comp, 2)
    side = lax.rem(low, 2)
    high = lax.rem(feat, highs)
    plane = lax.div(feat, highs)
    partner = (low * 2 + 1 - core, feat)
    odd = side == 1
    even = side == 0
    fed = low >= 2
    forwards = jnp.logical_and(odd, low < lows - 2)
    mine = plane < tiles
    my_rows = pl.multiple_of(core * half, 8)
    other_feat = plane * highs + 1 - high

    load_s = pltpu.make_async_copy(s_hbm.at[0], s_v, ld_sem.at[0])
    load_u = pltpu.make_async_copy(u_hbm, u_pad.at[pl.ds(group, group)], ld_sem.at[1])

    def set_rows(side_, core_):
        return pl.ds(pl.multiple_of((side_ * 2 + core_) * group, 8), group)

    own_group = set_rows(side, core)
    load_c = pltpu.make_async_copy(u_hbm, u_set.at[own_group], ld_sem.at[2])
    load_u.start()
    load_s.start()
    load_c.start()

    barrier = pltpu.get_barrier_semaphore()

    def plane_peer(d):
        q = lax.rem(plane * 2 + core + d, 2 * planes)
        p = lax.div(q, 2)
        return low * 2 + lax.rem(q, 2), p * highs + high

    def greet(d, carry):
        pl.semaphore_signal(barrier, inc=1, device_id=plane_peer(d), device_id_type=MESH)
        return carry

    across = (comp, other_feat)
    right = (comp + 2, feat)
    right_across = (comp + 2, other_feat)
    left = (comp - 2, feat)
    ahead = (comp + 4, feat)
    behind = (comp - 4, feat)
    line = highs * lows

    def along(d):
        z = lax.rem(high * lows + low + d + line, line)
        return lax.rem(z, lows) * 2 + core, plane * highs + lax.div(z, lows)

    def signal(semaphore, device):
        pl.semaphore_signal(semaphore, inc=1, device_id=device, device_id_type=MESH)

    signal(barrier, along(lows // 2))
    signal(barrier, along(-(lows // 2)))

    @pl.when(even)
    def _():
        signal(barrier, right)

    @pl.when(odd)
    def _():
        signal(barrier, along(lows // 2 - 1))
        signal(barrier, along(-(lows // 2) - 1))
        signal(barrier, left)

        @pl.when(fed)
        def _():
            pl.semaphore_signal(barrier, inc=1, device_id=behind, device_id_type=MESH)

    lax.fori_loop(1, 2 * planes, greet, 0)

    u_pad[0:group, :] = jnp.zeros((group, width), jnp.float32)
    u_pad[2 * group : 3 * group, :] = jnp.zeros((group, width), jnp.float32)
    load_u.wait()
    u_own = u_pad[group : 2 * group, :]
    squares = jnp.zeros((group, 128), jnp.float32)
    for b in range(blocks):
        piece = u_own[:, b * 128 : (b + 1) * 128]
        squares = squares + piece * piece
    squares = jnp.concatenate([squares, squares], axis=0)
    p_v[tiles - 1] = dot(jnp.ones((8, 128), jnp.float32), squares, 1, 1)
    load_s.wait()
    projected = dot(s_v[0:half, :], u_pad[group : 3 * group, :], 1, 1) + dot(
        s_v[half:rows, :], u_pad[0 : 2 * group, :], 1, 1
    )
    for t in range(tiles - 1):
        p_v[t] = projected[8 * t : 8 * t + 8, :]

    pl.semaphore_wait(
        barrier,
        2 * planes
        + jnp.where(even, 4, 2).astype(jnp.int32)
        + jnp.where(forwards, 1, 0).astype(jnp.int32),
    )

    signal(ready, along(lows // 2))
    signal(ready, along(-(lows // 2)))

    def scatter(t, wait):
        copy = pltpu.make_async_remote_copy(
            src_ref=p_v.at[t],
            dst_ref=rs_v.at[plane],
            send_sem=rs_send.at[t],
            recv_sem=rs_recv.at[plane],
            device_id=(comp, t * highs + high),
            device_id_type=MESH,
        )

        @pl.when(t != plane)
        def _():
            if wait:
                copy.wait_send()
            else:
                copy.start()

    def scatter_start(t, carry):
        scatter(t, False)
        return carry

    lax.fori_loop(0, tiles, scatter_start, 0)

    def lend(side_, core_, slot, device):
        where = set_rows(side_, core_)
        return pltpu.make_async_remote_copy(
            src_ref=u_set.at[where],
            dst_ref=u_set.at[where],
            send_sem=ux_send.at[slot],
            recv_sem=ux_recv.at[side_, core_],
            device_id=device,
            device_id_type=MESH,
        )

    def borrowed(side_, core_):
        landed(u_set.at[set_rows(side_, core_)], ux_recv.at[side_, core_])

    load_c.wait()
    lend(side, core, 0, partner).start()

    @pl.when(even)
    def _():
        lend(side, core, 1, right).start()

    def exchange(slot, device):
        return pltpu.make_async_remote_copy(
            src_ref=zs_v,
            dst_ref=zr_v.at[side, high],
            send_sem=z_send.at[slot],
            recv_sem=z_recv.at[side, high],
            device_id=device,
            device_id_type=MESH,
        )

    def crossed(side_, high_):
        landed(zr_v.at[side_, high_], z_recv.at[side_, high_])

    def spread(side_, d):
        return pltpu.make_async_remote_copy(
            src_ref=tot_v.at[side_],
            dst_ref=x_v.at[side_, core, plane],
            send_sem=ag_send.at[side_, d],
            recv_sem=ag_recv.at[side_, core, plane],
            device_id=plane_peer(d),
            device_id_type=MESH,
        )

    @pl.when(mine)
    def _():
        rs_v[plane] = p_v[plane]
        pl.semaphore_wait(ready, 2)

        def arrive(p, carry):
            @pl.when(p != plane)
            def _():
                landed(rs_v.at[p], rs_recv.at[p])

            return carry

        lax.fori_loop(0, planes, arrive, 0)
        total = rs_v[0]
        for p in range(1, planes):
            total = total + rs_v[p]
        zs_v[...] = total
        exchange(0, across).start()

        @pl.when(even)
        def _():
            exchange(1, right_across).start()
            exchange(2, right).start()

        zr_v[side, high] = total

    @pl.when(jnp.logical_not(mine))
    def _():
        pl.semaphore_wait(ready, 2)

    @pl.when(odd)
    def _():
        borrowed(0, core)
        lend(0, core, 1, partner).start()

    def spread_side(side_):
        tot_v[side_] = zr_v[side_, 0] + zr_v[side_, 1]

        def spread_start(d, carry):
            spread(side_, d).start()
            return carry

        lax.fori_loop(1, 2 * planes, spread_start, 0)
        x_v[side_, core, plane] = zr_v[side_, 0] + zr_v[side_, 1]

    @pl.when(mine)
    def _():
        crossed(side, 1 - high)
        spread_side(side)

        @pl.when(odd)
        def _():
            crossed(0, 0)
            crossed(0, 1)
            spread_side(0)

    borrowed(side, 1 - core)

    @pl.when(odd)
    def _():
        borrowed(0, 1 - core)

    def gather_side(side_):
        def gathered(i, carry):
            g = lax.div(i, tiles)
            t = lax.rem(i, tiles)

            @pl.when(jnp.logical_or(g != core, t != plane))
            def _():
                landed(x_v.at[side_, g, t], ag_recv.at[side_, g, t])

            return carry

        lax.fori_loop(0, 2 * tiles, gathered, 0)

    lane = lax.broadcasted_iota(jnp.int32, (8, 128), 1)
    eye = lax.broadcasted_iota(jnp.int32, (128, 128), 0) == lax.broadcasted_iota(jnp.int32, (128, 128), 1)

    def prepare(side_):
        gather_side(side_)
        scale0 = lax.rsqrt(x_v[side_, 0, tiles - 1] / features + epsilon)
        scale1 = lax.rsqrt(x_v[side_, 1, tiles - 1] / features + epsilon)
        scale_row = jnp.where(lane < group, scale0, scale1)
        for t in range(tiles - 1):
            x0 = x_v[side_, 0, t] * scale0 / root
            x1 = x_v[side_, 1, t] * scale1 / root
            a = jnp.where(lane < group, x0, pltpu.roll(x1, 64, 1))
            b = jnp.where(lane < group, pltpu.roll(x0, 64, 1), x1)
            xt_v[side_, pl.ds(8 * t, 8), :] = a
            xt_v[side_, pl.ds(half + 8 * t, 8), :] = b
        scale_col = jnp.sum(
            jnp.where(eye, jnp.broadcast_to(scale_row[0:1, :], (128, 128)), 0.0), axis=1, keepdims=True
        )
        v_v[side_] = u_set[128 * side_ : 128 * side_ + 128, :] * scale_col

    @pl.when(odd)
    def _():
        prepare(1)

    prepare(0)

    def add_own(b):
        columns = pl.ds(pl.multiple_of(b * 128, 128), 128)
        here = pl.ds(my_rows, half)
        own_v[b] = dot(xt_v[0, here, :], v_v[0, :, columns], 1, 0) + dot(
            xt_v[1, here, :], v_v[1, :, columns], 1, 0
        )

    @pl.when(jnp.logical_and(forwards, fed))
    def _():
        def each(b, carry):
            add_own(b)
            return carry

        lax.fori_loop(0, blocks, each, 0)

    my_group = pl.ds(pl.multiple_of(core * group, 8), group)

    def base():
        x_own = xt_v[side]
        xtt_v[...] = x_own.T
        x_mine = xtt_v[my_group, :]
        i = lax.broadcasted_iota(jnp.int32, (group, 128), 0) + core * group
        j = lax.broadcasted_iota(jnp.int32, (group, 128), 1)
        pairs = jnp.where(j < i, dot(x_mine, x_own, 1, 0) / rows, 0.0)
        pull = dot(x_mine, s_v[...], 1, 0) * (root / rows) - dot(pairs, v_v[side], 1, 0)
        new_v[...] = v_v[side, my_group, :] + step_rate * pull

        @pl.when(odd)
        def _():
            cross = dot(x_mine, xt_v[0], 1, 0) / rows
            new_v[...] = new_v[...] - step_rate * dot(cross, v_v[0], 1, 0)

    starts = low == 1

    @pl.when(jnp.logical_not(starts))
    def _():
        base()

    def hop(b, s):
        i = b * subs + s
        here = pl.ds(pl.multiple_of(my_rows + s * sub, 8), sub)
        there = pl.ds(pl.multiple_of(s * sub, 8), sub)

        def send(src, sem, arrival, device):
            return pltpu.make_async_remote_copy(
                src_ref=src,
                dst_ref=in_v.at[b, here],
                send_sem=sem.at[i],
                recv_sem=arrival.at[i],
                device_id=device,
                device_id_type=MESH,
            )

        forward = send(o_v.at[b, there], ch_send, ch_recv, ahead)
        back = send(in_v.at[b, here], lf_send, ch_recv, left)
        relay = send(in_v.at[b, here], rl_send, rl_recv, partner)
        return here, there, forward, back, relay

    def finish(b):
        def arrived(s, carry):
            other = pl.ds(pl.multiple_of((1 - core) * half + s * sub, 8), sub)
            landed(in_v.at[b, other], rl_recv.at[b * subs + s])
            return carry

        lax.fori_loop(0, subs, arrived, 0)
        columns = pl.ds(pl.multiple_of(b * 128, 128), 128)
        new_v[:, columns] = new_v[:, columns] - dot(xtt_v[my_group, :], in_v[b], 1, 0) * (step_rate / rows)

    def chain(b, carry):
        @pl.when(starts)
        def _():
            add_own(b)

        def one(s, carry):
            here, there, forward, back, relay = hop(b, s)

            @pl.when(fed)
            def _():
                landed(in_v.at[b, here], ch_recv.at[b * subs + s])

                @pl.when(forwards)
                def _():
                    o_v[b, there] = in_v[b, here] + own_v[b, there]
                    forward.start()

                @pl.when(odd)
                def _():
                    back.start()

                relay.start()

            @pl.when(starts)
            def _():
                o_v[b, there] = own_v[b, there]
                forward.start()

            return carry

        lax.fori_loop(0, subs, one, 0)

        @pl.when(jnp.logical_and(jnp.logical_and(fed, jnp.logical_not(forwards)), b > 0))
        def _():
            finish(b - 1)

        return carry

    lax.fori_loop(0, blocks, chain, 0)

    @pl.when(jnp.logical_and(fed, jnp.logical_not(forwards)))
    def _():
        finish(blocks - 1)

    @pl.when(starts)
    def _():
        base()

    @pl.when(jnp.logical_and(fed, forwards))
    def _():
        def finish_all(b, carry):
            finish(b)
            return carry

        lax.fori_loop(0, blocks, finish_all, 0)

    squares = jnp.zeros((group, 128), jnp.float32)
    for b in range(blocks):
        piece = new_v[:, b * 128 : (b + 1) * 128]
        squares = squares + piece * piece
    column = jnp.sum(squares, axis=1, keepdims=True)
    eye_half = lax.broadcasted_iota(jnp.int32, (group, 128), 0) == lax.broadcasted_iota(
        jnp.int32, (group, 128), 1
    )
    fin_v[feat] = jnp.sum(jnp.where(eye_half, column, 0.0), axis=0, keepdims=True)

    def tell(d):
        q = lax.rem(feat + d, feats)
        return pltpu.make_async_remote_copy(
            src_ref=fin_v.at[feat],
            dst_ref=fin_v.at[feat],
            send_sem=fin_send.at[d],
            recv_sem=fin_recv.at[feat],
            device_id=(comp, q),
            device_id_type=MESH,
        )

    def tell_start(d, carry):
        tell(d).start()
        return carry

    lax.fori_loop(1, feats, tell_start, 0)
    store = pltpu.make_async_copy(new_v, out_hbm, ld_sem.at[0])
    store.start()

    def scatter_end(t, carry):
        scatter(t, True)
        return carry

    lax.fori_loop(0, tiles, scatter_end, 0)
    lend(side, core, 0, partner).wait_send()

    @pl.when(even)
    def _():
        lend(side, core, 1, right).wait_send()

    @pl.when(odd)
    def _():
        lend(0, core, 1, partner).wait_send()

    def spread_end_of(side_):
        def spread_end(d, carry):
            spread(side_, d).wait_send()
            return carry

        lax.fori_loop(1, 2 * planes, spread_end, 0)

    @pl.when(mine)
    def _():
        exchange(0, across).wait_send()

        @pl.when(even)
        def _():
            exchange(1, right_across).wait_send()
            exchange(2, right).wait_send()

        spread_end_of(side)

        @pl.when(odd)
        def _():
            spread_end_of(0)

    def chain_end(i, carry):
        here, there, forward, back, relay = hop(lax.div(i, subs), lax.rem(i, subs))

        @pl.when(forwards)
        def _():
            forward.wait_send()

        @pl.when(fed)
        def _():
            relay.wait_send()

            @pl.when(odd)
            def _():
                back.wait_send()

        return carry

    lax.fori_loop(0, blocks * subs, chain_end, 0)

    def told(d, carry):
        q = lax.rem(feat + d, feats)
        landed(fin_v.at[q], fin_recv.at[q])
        return carry

    lax.fori_loop(1, feats, told, 0)
    total = fin_v[0]
    for q in range(1, feats):
        total = total + fin_v[q]
    scale_ref[...] = jnp.broadcast_to(
        lax.rsqrt(
            jnp.sum(jnp.where(eye_half, jnp.broadcast_to(total, (group, 128)), 0.0), axis=1, keepdims=True)
            / features
            + epsilon
        ),
        (group, width),
    )

    def tell_end(d, carry):
        tell(d).wait_send()
        return carry

    lax.fori_loop(1, feats, tell_end, 0)
    store.wait()


def step(planes, highs, lows, sub, samples, start_vectors):
    _, rows, width = samples.shape
    group = start_vectors.shape[0]
    feats = planes * highs
    half = rows // 2
    tiles = half // 8 + 1
    blocks = width // 128
    chunks = blocks * (half // sub)
    dma = pltpu.SemaphoreType.DMA
    f32 = jnp.float32
    updated, scale = pl.pallas_call(
        functools.partial(kernel, planes, highs, lows, sub, width * feats),
        out_shape=(
            jax.ShapeDtypeStruct((group, width), f32),
            jax.ShapeDtypeStruct((group, width), f32),
        ),
        in_specs=[pl.BlockSpec(memory_space=pl.ANY)] * 2,
        out_specs=(pl.BlockSpec(memory_space=pl.ANY), pl.BlockSpec(memory_space=pltpu.VMEM)),
        scratch_shapes=[
            pltpu.VMEM((group, width), f32),
            pltpu.VMEM((rows, width), f32),
            pltpu.VMEM((3 * group, width), f32),
            pltpu.VMEM((4 * group, width), f32),
            pltpu.VMEM((tiles, 8, 128), f32),
            pltpu.VMEM((planes, 8, 128), f32),
            pltpu.VMEM((8, 128), f32),
            pltpu.VMEM((2, 2, 8, 128), f32),
            pltpu.VMEM((2, 8, 128), f32),
            pltpu.VMEM((2, 2, tiles, 8, 128), f32),
            pltpu.VMEM((2, 2 * group, width), f32),
            pltpu.VMEM((2, rows, 128), f32),
            pltpu.VMEM((128, rows), f32),
            pltpu.VMEM((blocks, half, 128), f32),
            pltpu.VMEM((blocks, rows, 128), f32),
            pltpu.VMEM((blocks, half, 128), f32),
            pltpu.VMEM((feats, 1, 128), f32),
            dma((3,)),
            dma((2,)),
            dma((2, 2)),
            dma((tiles,)),
            dma((planes,)),
            dma((3,)),
            dma((2, 2)),
            dma((2, 2 * planes)),
            dma((2, 2, tiles)),
            dma((chunks,)),
            dma((chunks,)),
            dma((chunks,)),
            dma((chunks,)),
            dma((chunks,)),
            dma((feats,)),
            dma((feats,)),
            pltpu.SemaphoreType.REGULAR,
        ],
        compiler_params=pltpu.CompilerParams(collective_id=0, has_side_effects=True, vmem_limit_bytes=54700 * 1024),
    )(samples, start_vectors)
    return updated * scale


def solution(mesh, sub=SUB, planes=16, highs=2, lows=8):
    in_specs = (P(None, None, "feat"), P("comp", "feat"))
    return jax.shard_map(
        functools.partial(step, planes, highs, lows, sub),
        mesh=mesh,
        in_specs=in_specs,
        out_specs=P("comp", "feat"),
        check_vma=False,
    )
```

```python
import functools
import math

import jax
import jax.numpy as jnp
from jax import lax
from jax.experimental import pallas as pl
from jax.experimental.pallas import tpu as pltpu
from jax.sharding import PartitionSpec as P

MESH = pl.DeviceIdType.MESH
step_rate = 0.1
epsilon = 1e-06
highest = lax.Precision.HIGHEST

SUB = 24
OWNERS = (2, 2, 8, 8, 5, 7, 13, 15, 1, 3, 4, 12, 0)


def dot(a, b, ca, cb):
    return lax.dot_general(
        a, b, (((ca,), (cb,)), ((), ())), precision=highest, preferred_element_type=jnp.float32
    )


def landed(ref, sem):
    pltpu.make_async_copy(ref, ref, sem).wait()


def kernel(
    planes, highs, lows, sub, owners, features,
    s_hbm, u_hbm, out_hbm, scale_ref,
    new_v, s_v, u_pad, u_set, p_v, rs_v, zs_v, zr_v, tot_v, x_v, v_v, xt_v, xtt_v, own_v, in_v, o_v, fin_v, sent_v,
    ld_sem, ux_send, ux_recv, rs_send, rs_recv, z_send, z_recv, ag_send, ag_recv, xr_send, xr_recv,
    ch_send, lf_send, ch_recv, rl_send, rl_recv, fin_send, fin_recv, ready,
):
    rows, width = s_v.shape
    half = rows // 2
    tiles = half // 8 + 1
    group = 64
    blocks = width // 128
    subs = half // sub
    feats = planes * highs
    root = math.sqrt(features)

    comp = lax.axis_index("comp")
    feat = lax.axis_index("feat")
    core = lax.rem(comp, 2)
    low = lax.div(comp, 2)
    side = lax.rem(low, 2)
    high = lax.rem(feat, highs)
    plane = lax.div(feat, highs)
    partner = (low * 2 + 1 - core, feat)
    odd = side == 1
    even = side == 0
    fed = low >= 2
    single = low >= lows - 2
    forwards = jnp.logical_or(jnp.logical_and(odd, jnp.logical_not(single)), low == lows - 2)
    lends = jnp.logical_and(even, jnp.logical_not(single))
    heads = jnp.logical_and(odd, jnp.logical_not(single))
    slot_of = [owners[:t].count(owners[t]) for t in range(tiles)]
    slots = max(slot_of) + 1
    first_tile, count = 0, 0
    for t in range(tiles):
        owned = plane == owners[t]
        count = count + jnp.where(owned, 1, 0).astype(jnp.int32)
        if slot_of[t] == 0:
            first_tile = first_tile + jnp.where(owned, t, 0).astype(jnp.int32)
    side_len = math.isqrt(planes)
    reach = side_len // 2
    here_x = lax.div(plane, side_len)
    here_y = lax.rem(plane, side_len)

    def plane_at(k):
        x = lax.rem(here_x + reach + lax.div(k, side_len), side_len)
        y = lax.rem(here_y + reach + lax.rem(k, side_len), side_len)
        return x * side_len + y

    itself = reach * side_len + reach
    my_rows = pl.multiple_of(core * half, 8)
    other_feat = plane * highs + 1 - high

    load_s = pltpu.make_async_copy(s_hbm.at[0], s_v, ld_sem.at[0])
    load_u = pltpu.make_async_copy(u_hbm, u_pad.at[pl.ds(group, group)], ld_sem.at[1])

    def set_rows(side_, core_):
        return pl.ds(pl.multiple_of((side_ * 2 + core_) * group, 8), group)

    own_group = set_rows(side, core)
    load_c = pltpu.make_async_copy(u_hbm, u_set.at[own_group], ld_sem.at[2])
    load_u.start()
    load_s.start()
    load_c.start()

    barrier = pltpu.get_barrier_semaphore()

    def plane_peer(d):
        q = lax.rem(plane * 2 + core + d, 2 * planes)
        p = lax.div(q, 2)
        return low * 2 + lax.rem(q, 2), p * highs + high

    def greet(d, carry):
        pl.semaphore_signal(barrier, inc=1, device_id=plane_peer(d), device_id_type=MESH)
        return carry

    across = (comp, other_feat)
    right = (comp + 2, feat)
    right_across = (comp + 2, other_feat)
    left = (comp - 2, feat)
    ahead = (comp + 4, feat)
    behind = (comp - 4, feat)
    line = highs * lows

    def along(d):
        z = lax.rem(high * lows + low + d + line, line)
        return lax.rem(z, lows) * 2 + core, plane * highs + lax.div(z, lows)

    def signal(semaphore, device):
        pl.semaphore_signal(semaphore, inc=1, device_id=device, device_id_type=MESH)

    signal(barrier, along(lows // 2))
    signal(barrier, along(-(lows // 2)))

    @pl.when(even)
    def _():
        signal(barrier, right)

    @pl.when(odd)
    def _():
        signal(barrier, along(lows // 2 - 1))
        signal(barrier, along(-(lows // 2) - 1))
        signal(barrier, left)

        @pl.when(jnp.logical_and(fed, heads))
        def _():
            signal(barrier, behind)

    @pl.when(low == lows - 2)
    def _():
        signal(barrier, left)

    lax.fori_loop(1, 2 * planes, greet, 0)

    u_pad[0:group, :] = jnp.zeros((group, width), jnp.float32)
    u_pad[2 * group : 3 * group, :] = jnp.zeros((group, width), jnp.float32)
    load_u.wait()
    u_own = u_pad[group : 2 * group, :]
    squares = jnp.zeros((group, 128), jnp.float32)
    for b in range(blocks):
        piece = u_own[:, b * 128 : (b + 1) * 128]
        squares = squares + piece * piece
    squares = jnp.concatenate([squares, squares], axis=0)
    p_v[tiles - 1] = dot(jnp.ones((8, 128), jnp.float32), squares, 1, 1)
    load_s.wait()
    projected = dot(s_v[0:half, :], u_pad[group : 3 * group, :], 1, 1) + dot(
        s_v[half:rows, :], u_pad[0 : 2 * group, :], 1, 1
    )
    for t in range(tiles - 1):
        p_v[t] = projected[8 * t : 8 * t + 8, :]

    pl.semaphore_wait(
        barrier,
        2 * planes
        + jnp.where(even, 4, 2).astype(jnp.int32)
        + jnp.where(heads, 1, 0).astype(jnp.int32),
    )

    signal(ready, along(lows // 2))
    signal(ready, along(-(lows // 2)))

    for t in range(tiles):

        @pl.when(plane != owners[t])
        def _():
            pltpu.make_async_remote_copy(
                src_ref=p_v.at[t],
                dst_ref=rs_v.at[slot_of[t], plane],
                send_sem=rs_send,
                recv_sem=rs_recv,
                device_id=(comp, owners[t] * highs + high),
                device_id_type=MESH,
            ).start()

    def lend(side_, core_, slot, device):
        where = set_rows(side_, core_)
        return pltpu.make_async_remote_copy(
            src_ref=u_set.at[where],
            dst_ref=u_set.at[where],
            send_sem=ux_send.at[slot],
            recv_sem=ux_recv.at[side_, core_],
            device_id=device,
            device_id_type=MESH,
        )

    def borrowed(side_, core_):
        landed(u_set.at[set_rows(side_, core_)], ux_recv.at[side_, core_])

    load_c.wait()
    lend(side, core, 0, partner).start()

    @pl.when(lends)
    def _():
        lend(side, core, 1, right).start()

    def exchange(n, device):
        return pltpu.make_async_remote_copy(
            src_ref=zs_v.at[pl.ds(0, n)],
            dst_ref=zr_v.at[side, high, pl.ds(0, n)],
            send_sem=z_send,
            recv_sem=z_recv.at[side, high],
            device_id=device,
            device_id_type=MESH,
        )

    def crossed(n, side_, high_):
        landed(zr_v.at[side_, high_, pl.ds(0, n)], z_recv.at[side_, high_])

    pl.semaphore_wait(ready, 2)
    for n in range(1, slots + 1):

        @pl.when(count == n)
        def _():
            for slot in range(n):
                rs_v[slot, plane] = p_v[first_tile + slot]
            landed(rs_v.at[pl.ds(0, n), pl.ds(0, planes - 1)], rs_recv)
            for slot in range(n):
                total = rs_v[slot, 0]
                for p in range(1, planes):
                    total = total + rs_v[slot, p]
                zs_v[slot] = total
            exchange(n, across).start()

            @pl.when(lends)
            def _():
                exchange(n, right_across).start()
                exchange(n, right).start()

            for slot in range(n):
                zr_v[side, high, slot] = zs_v[slot]

    @pl.when(heads)
    def _():
        borrowed(0, core)
        lend(0, core, 1, partner).start()

    place = core * tiles + first_tile

    def spread_side(n, side_):
        for slot in range(n):
            total = zr_v[side_, 0, slot] + zr_v[side_, 1, slot]
            tot_v[side_, slot] = total
            x_v[side_, place + slot] = total

        def spread_start(k, carry):
            @pl.when(k != itself)
            def _():
                pltpu.make_async_remote_copy(
                    src_ref=tot_v.at[side_, pl.ds(0, n)],
                    dst_ref=x_v.at[side_, pl.ds(place, n)],
                    send_sem=ag_send.at[side_],
                    recv_sem=ag_recv.at[side_],
                    device_id=(comp, plane_at(k) * highs + high),
                    device_id_type=MESH,
                ).start()

            return carry

        lax.fori_loop(0, planes, spread_start, 0)

    for n in range(1, slots + 1):

        @pl.when(count == n)
        def _():
            crossed(n, side, 1 - high)
            spread_side(n, side)

            @pl.when(heads)
            def _():
                crossed(n, 0, 0)
                crossed(n, 0, 1)
                spread_side(n, 0)

    borrowed(side, 1 - core)

    @pl.when(heads)
    def _():
        borrowed(0, 1 - core)

    def pass_on(side_):
        tiles_here = pl.ds(core * tiles, tiles)
        return pltpu.make_async_remote_copy(
            src_ref=x_v.at[side_, tiles_here],
            dst_ref=x_v.at[side_, tiles_here],
            send_sem=xr_send.at[side_],
            recv_sem=xr_recv.at[side_],
            device_id=partner,
            device_id_type=MESH,
        )

    def collect(side_):
        for n in range(slots + 1):

            @pl.when(count == n)
            def _():
                landed(x_v.at[side_, pl.ds(0, tiles - n)], ag_recv.at[side_])

        pass_on(side_).start()

    collect(side)

    @pl.when(heads)
    def _():
        collect(0)

    def gather_side(side_):
        landed(x_v.at[side_, pl.ds((1 - core) * tiles, tiles)], xr_recv.at[side_])

    lane = lax.broadcasted_iota(jnp.int32, (8, 128), 1)
    eye = lax.broadcasted_iota(jnp.int32, (128, 128), 0) == lax.broadcasted_iota(jnp.int32, (128, 128), 1)

    def prepare(side_):
        gather_side(side_)
        scale0 = lax.rsqrt(x_v[side_, tiles - 1] / features + epsilon)
        scale1 = lax.rsqrt(x_v[side_, 2 * tiles - 1] / features + epsilon)
        scale_row = jnp.where(lane < group, scale0, scale1)
        for t in range(tiles - 1):
            x0 = x_v[side_, t] * scale0 / root
            x1 = x_v[side_, tiles + t] * scale1 / root
            a = jnp.where(lane < group, x0, pltpu.roll(x1, 64, 1))
            b = jnp.where(lane < group, pltpu.roll(x0, 64, 1), x1)
            xt_v[side_, pl.ds(8 * t, 8), :] = a
            xt_v[side_, pl.ds(half + 8 * t, 8), :] = b
        scale_col = jnp.sum(
            jnp.where(eye, jnp.broadcast_to(scale_row[0:1, :], (128, 128)), 0.0), axis=1, keepdims=True
        )
        v_v[side_] = u_set[128 * side_ : 128 * side_ + 128, :] * scale_col

    @pl.when(odd)
    def _():
        prepare(1)

    @pl.when(jnp.logical_or(even, heads))
    def _():
        prepare(0)

    def add_own(b):
        columns = pl.ds(pl.multiple_of(b * 128, 128), 128)
        here = pl.ds(my_rows, half)
        own_v[b] = dot(xt_v[0, here, :], v_v[0, :, columns], 1, 0)

        @pl.when(heads)
        def _():
            own_v[b] = own_v[b] + dot(xt_v[1, here, :], v_v[1, :, columns], 1, 0)

    @pl.when(jnp.logical_and(forwards, fed))
    def _():
        def each(b, carry):
            add_own(b)
            return carry

        lax.fori_loop(0, blocks, each, 0)

    my_group = pl.ds(pl.multiple_of(core * group, 8), group)

    def base():
        x_own = xt_v[side]
        xtt_v[...] = x_own.T
        x_mine = xtt_v[my_group, :]
        i = lax.broadcasted_iota(jnp.int32, (group, 128), 0) + core * group
        j = lax.broadcasted_iota(jnp.int32, (group, 128), 1)
        pairs = jnp.where(j < i, dot(x_mine, x_own, 1, 0) / rows, 0.0)
        pull = dot(x_mine, s_v[...], 1, 0) * (root / rows) - dot(pairs, v_v[side], 1, 0)
        new_v[...] = v_v[side, my_group, :] + step_rate * pull

        @pl.when(heads)
        def _():
            cross = dot(x_mine, xt_v[0], 1, 0) / rows
            new_v[...] = new_v[...] - step_rate * dot(cross, v_v[0], 1, 0)

    starts = low == 1
    late = jnp.logical_and(heads, low < 5)

    @pl.when(jnp.logical_not(late))
    def _():
        base()

    def hop(b, s):
        i = b * subs + s
        here = pl.ds(pl.multiple_of(my_rows + s * sub, 8), sub)
        there = pl.ds(pl.multiple_of(s * sub, 8), sub)

        def send(src, sem, arrival, device):
            return pltpu.make_async_remote_copy(
                src_ref=src,
                dst_ref=in_v.at[b, here],
                send_sem=sem,
                recv_sem=arrival,
                device_id=device,
                device_id_type=MESH,
            )

        target = comp + jnp.where(low < lows - 3, 4, 2).astype(jnp.int32)
        forward = send(o_v.at[b, there], ch_send, ch_recv.at[i], (target, feat))
        back = send(in_v.at[b, here], lf_send, ch_recv.at[i], left)
        relay = send(in_v.at[b, here], rl_send, rl_recv.at[b], partner)
        return here, there, forward, back, relay

    def finish(b):
        other = pl.ds(pl.multiple_of((1 - core) * half, 8), half)
        landed(in_v.at[b, other], rl_recv.at[b])
        columns = pl.ds(pl.multiple_of(b * 128, 128), 128)
        new_v[:, columns] = new_v[:, columns] - dot(xtt_v[my_group, :], in_v[b], 1, 0) * (step_rate / rows)

    def chain(b, carry):
        @pl.when(starts)
        def _():
            add_own(b)

        def one(s, carry):
            here, there, forward, back, relay = hop(b, s)

            @pl.when(fed)
            def _():
                landed(in_v.at[b, here], ch_recv.at[b * subs + s])

                @pl.when(forwards)
                def _():
                    o_v[b, there] = in_v[b, here] + own_v[b, there]
                    forward.start()

                @pl.when(heads)
                def _():
                    back.start()

                relay.start()

            @pl.when(starts)
            def _():
                o_v[b, there] = own_v[b, there]
                forward.start()

            return carry

        lax.fori_loop(0, subs, one, 0)

        @pl.when(jnp.logical_and(jnp.logical_and(fed, jnp.logical_not(forwards)), b > 0))
        def _():
            finish(b - 1)

        return carry

    lax.fori_loop(0, blocks, chain, 0)

    @pl.when(jnp.logical_and(fed, jnp.logical_not(forwards)))
    def _():
        finish(blocks - 1)

    @pl.when(late)
    def _():
        base()

    @pl.when(jnp.logical_and(fed, forwards))
    def _():
        def finish_all(b, carry):
            finish(b)
            return carry

        lax.fori_loop(0, blocks, finish_all, 0)

    squares = jnp.zeros((group, 128), jnp.float32)
    for b in range(blocks):
        piece = new_v[:, b * 128 : (b + 1) * 128]
        squares = squares + piece * piece
    column = jnp.sum(squares, axis=1, keepdims=True)
    eye_half = lax.broadcasted_iota(jnp.int32, (group, 128), 0) == lax.broadcasted_iota(
        jnp.int32, (group, 128), 1
    )
    fin_v[feat] = jnp.sum(jnp.where(eye_half, column, 0.0), axis=0, keepdims=True)

    def tell(k, high_):
        pltpu.make_async_remote_copy(
            src_ref=fin_v.at[feat],
            dst_ref=fin_v.at[feat],
            send_sem=fin_send,
            recv_sem=fin_recv,
            device_id=(comp, plane_at(k) * highs + high_),
            device_id_type=MESH,
        ).start()

    def tell_across(k, carry):
        tell(k, 1 - high)
        return carry

    def tell_plane(k, carry):
        @pl.when(k != itself)
        def _():
            tell(k, high)

        return carry

    lax.fori_loop(0, planes, tell_across, 0)
    lax.fori_loop(0, planes, tell_plane, 0)
    store = pltpu.make_async_copy(new_v, out_hbm, ld_sem.at[0])
    store.start()

    for n in range(slots + 1):

        @pl.when(count == n)
        def _():
            landed(sent_v.at[pl.ds(0, tiles - n)], rs_send)

    lend(side, core, 0, partner).wait_send()

    @pl.when(lends)
    def _():
        lend(side, core, 1, right).wait_send()

    @pl.when(heads)
    def _():
        lend(0, core, 1, partner).wait_send()

    pass_on(side).wait_send()

    @pl.when(heads)
    def _():
        pass_on(0).wait_send()

    for n in range(1, slots + 1):

        @pl.when(count == n)
        def _():
            @pl.when(lends)
            def _():
                landed(sent_v.at[pl.ds(0, 3 * n)], z_send)

            @pl.when(jnp.logical_not(lends))
            def _():
                landed(sent_v.at[pl.ds(0, n)], z_send)

            landed(sent_v.at[pl.ds(0, n * (planes - 1))], ag_send.at[side])

            @pl.when(heads)
            def _():
                landed(sent_v.at[pl.ds(0, n * (planes - 1))], ag_send.at[0])

    @pl.when(forwards)
    def _():
        landed(o_v, ch_send)

    @pl.when(fed)
    def _():
        landed(o_v, rl_send)

        @pl.when(heads)
        def _():
            landed(o_v, lf_send)

    landed(fin_v.at[pl.ds(0, feats - 1)], fin_recv)
    total = fin_v[0]
    for q in range(1, feats):
        total = total + fin_v[q]
    scale_ref[...] = jnp.broadcast_to(
        lax.rsqrt(
            jnp.sum(jnp.where(eye_half, jnp.broadcast_to(total, (group, 128)), 0.0), axis=1, keepdims=True)
            / features
            + epsilon
        ),
        (group, width),
    )

    landed(fin_v.at[pl.ds(0, feats - 1)], fin_send)
    store.wait()


def step(planes, highs, lows, sub, owners, samples, start_vectors):
    _, rows, width = samples.shape
    group = start_vectors.shape[0]
    feats = planes * highs
    half = rows // 2
    tiles = half // 8 + 1
    blocks = width // 128
    chunks = blocks * (half // sub)
    slots = max(owners.count(plane) for plane in owners)
    dma = pltpu.SemaphoreType.DMA
    f32 = jnp.float32
    updated, scale = pl.pallas_call(
        functools.partial(kernel, planes, highs, lows, sub, owners, width * feats),
        out_shape=(
            jax.ShapeDtypeStruct((group, width), f32),
            jax.ShapeDtypeStruct((group, width), f32),
        ),
        in_specs=[pl.BlockSpec(memory_space=pl.ANY)] * 2,
        out_specs=(pl.BlockSpec(memory_space=pl.ANY), pl.BlockSpec(memory_space=pltpu.VMEM)),
        scratch_shapes=[
            pltpu.VMEM((group, width), f32),
            pltpu.VMEM((rows, width), f32),
            pltpu.VMEM((3 * group, width), f32),
            pltpu.VMEM((4 * group, width), f32),
            pltpu.VMEM((tiles, 8, 128), f32),
            pltpu.VMEM((slots, planes, 8, 128), f32),
            pltpu.VMEM((slots, 8, 128), f32),
            pltpu.VMEM((2, 2, slots, 8, 128), f32),
            pltpu.VMEM((2, slots, 8, 128), f32),
            pltpu.VMEM((2, 2 * tiles, 8, 128), f32),
            pltpu.VMEM((2, 2 * group, width), f32),
            pltpu.VMEM((2, rows, 128), f32),
            pltpu.VMEM((128, rows), f32),
            pltpu.VMEM((blocks, half, 128), f32),
            pltpu.VMEM((blocks, rows, 128), f32),
            pltpu.VMEM((blocks, half, 128), f32),
            pltpu.VMEM((feats, 1, 128), f32),
            pltpu.VMEM((slots * planes, 8, 128), f32),
            dma((3,)),
            dma((2,)),
            dma((2, 2)),
            dma,
            dma,
            dma,
            dma((2, 2)),
            dma((2,)),
            dma((2,)),
            dma((2,)),
            dma((2,)),
            dma,
            dma,
            dma((chunks,)),
            dma,
            dma((blocks,)),
            dma,
            dma,
            pltpu.SemaphoreType.REGULAR,
        ],
        compiler_params=pltpu.CompilerParams(collective_id=0, has_side_effects=True, vmem_limit_bytes=54700 * 1024),
    )(samples, start_vectors)
    return updated * scale


def solution(mesh, sub=SUB, owners=OWNERS, planes=16, highs=2, lows=8):
    in_specs = (P(None, None, "feat"), P("comp", "feat"))
    return jax.shard_map(
        functools.partial(step, planes, highs, lows, sub, owners),
        mesh=mesh,
        in_specs=in_specs,
        out_specs=P("comp", "feat"),
        check_vma=False,
    )
```

```python
import functools
import math

import jax
import jax.numpy as jnp
from jax import lax
from jax.experimental import pallas as pl
from jax.experimental.pallas import tpu as pltpu
from jax.sharding import PartitionSpec as P

MESH = pl.DeviceIdType.MESH
step_rate = 0.1
epsilon = 1e-06
highest = lax.Precision.HIGHEST

SUB = 24
OWNERS = (10, 10, 6, 6, 9, 11, 14, 2, 5, 7, 8, 13, 15)


def dot_exact(a, b, ca, cb):
    return lax.dot_general(
        a, b, (((ca,), (cb,)), ((), ())), precision=highest, preferred_element_type=jnp.float32
    )


def split(a):
    high = a.astype(jnp.bfloat16)
    return high, (a - high.astype(jnp.float32)).astype(jnp.bfloat16)


def dot(a, b, ca, cb):
    a_high, a_low = split(a)
    b_high, b_low = split(b)

    def product(x, y):
        return lax.dot_general(x, y, (((ca,), (cb,)), ((), ())), preferred_element_type=jnp.float32)

    return product(a_high, b_high) + (product(a_high, b_low) + product(a_low, b_high))


def landed(ref, sem):
    pltpu.make_async_copy(ref, ref, sem).wait()


def kernel(
    planes, highs, lows, sub, owners, features,
    s_hbm, u_hbm, out_hbm, scale_ref,
    new_v, s_v, u_pad, u_set, p_v, rs_v, zs_v, zr_v, tot_v, x_v, v_v, xt_v, xs_v, xtt_v, own_v, in_v, o_v, fin_v, sent_v,
    ld_sem, ux_send, ux_recv, rs_send, rs_recv, z_send, z_recv, ag_send, ag_recv, xr_send, xr_recv,
    ch_send, lf_send, ch_recv, rl_send, rl_recv, fin_send, fin_recv, ready,
):
    rows, width = s_v.shape
    half = rows // 2
    tiles = half // 8 + 1
    group = 64
    blocks = width // 128
    subs = half // sub
    feats = planes * highs
    root = math.sqrt(features)

    comp = lax.axis_index("comp")
    feat = lax.axis_index("feat")
    core = lax.rem(comp, 2)
    low = lax.div(comp, 2)
    side = lax.rem(low, 2)
    high = lax.rem(feat, highs)
    plane = lax.div(feat, highs)
    partner = (low * 2 + 1 - core, feat)
    odd = side == 1
    even = side == 0
    fed = low >= 2
    single = low >= lows - 2
    forwards = jnp.logical_or(jnp.logical_and(odd, jnp.logical_not(single)), low == lows - 2)
    lends = jnp.logical_and(even, jnp.logical_not(single))
    heads = jnp.logical_and(odd, jnp.logical_not(single))
    slot_of = [owners[:t].count(owners[t]) for t in range(tiles)]
    slots = max(slot_of) + 1
    first_tile, count = 0, 0
    for t in range(tiles):
        owned = plane == owners[t]
        count = count + jnp.where(owned, 1, 0).astype(jnp.int32)
        if slot_of[t] == 0:
            first_tile = first_tile + jnp.where(owned, t, 0).astype(jnp.int32)
    side_len = math.isqrt(planes)
    reach = side_len // 2
    here_x = lax.div(plane, side_len)
    here_y = lax.rem(plane, side_len)

    def plane_at(k):
        x = lax.rem(here_x + reach + lax.div(k, side_len), side_len)
        y = lax.rem(here_y + reach + lax.rem(k, side_len), side_len)
        return x * side_len + y

    itself = reach * side_len + reach
    my_rows = pl.multiple_of(core * half, 8)
    other_feat = plane * highs + 1 - high

    load_s = [
        pltpu.make_async_copy(s_hbm.at[0, pl.ds(r, half)], s_v.at[pl.ds(r, half)], ld_sem.at[n])
        for n, r in ((0, 0), (3, half))
    ]
    load_u = pltpu.make_async_copy(u_hbm, u_pad.at[pl.ds(group, group)], ld_sem.at[1])

    def set_rows(side_, core_):
        return pl.ds(pl.multiple_of((side_ * 2 + core_) * group, 8), group)

    own_group = set_rows(side, core)
    load_c = pltpu.make_async_copy(u_hbm, u_set.at[own_group], ld_sem.at[2])
    load_u.start()
    load_s[0].start()
    load_s[1].start()
    load_c.start()

    barrier = pltpu.get_barrier_semaphore()

    across = (comp, other_feat)
    right = (comp + 2, feat)
    right_across = (comp + 2, other_feat)
    left = (comp - 2, feat)
    ahead = (comp + 4, feat)
    behind = (comp - 4, feat)
    line = highs * lows

    def along(d):
        z = lax.rem(high * lows + low + d + line, line)
        return lax.rem(z, lows) * 2 + core, plane * highs + lax.div(z, lows)

    def signal(semaphore, device):
        pl.semaphore_signal(semaphore, inc=1, device_id=device, device_id_type=MESH)

    @pl.when(count > 0)
    def _():
        def greet(k, carry):
            @pl.when(k != itself)
            def _():
                signal(barrier, (comp, plane_at(k) * highs + high))

            return carry

        lax.fori_loop(0, planes, greet, 0)

    signal(barrier, along(lows // 2))
    signal(barrier, along(-(lows // 2)))

    @pl.when(even)
    def _():
        signal(barrier, right)

    @pl.when(odd)
    def _():
        signal(barrier, along(lows // 2 - 1))
        signal(barrier, along(-(lows // 2) - 1))
        signal(barrier, left)

        @pl.when(jnp.logical_and(fed, heads))
        def _():
            signal(barrier, behind)

    @pl.when(low == lows - 2)
    def _():
        signal(barrier, left)

    signal(barrier, partner)

    u_pad[0:group, :] = jnp.zeros((group, width), jnp.float32)
    u_pad[2 * group : 3 * group, :] = jnp.zeros((group, width), jnp.float32)
    load_u.wait()
    u_own = u_pad[group : 2 * group, :]
    squares = jnp.zeros((group, 128), jnp.float32)
    for b in range(blocks):
        piece = u_own[:, b * 128 : (b + 1) * 128]
        squares = squares + piece * piece
    squares = jnp.concatenate([squares, squares], axis=0)
    p_v[tiles - 1] = dot_exact(jnp.ones((8, 128), jnp.float32), squares, 1, 1)
    load_s[0].wait()
    projected = dot(s_v[0:half, :], u_pad[group : 3 * group, :], 1, 1)
    load_s[1].wait()
    projected = projected + dot(s_v[half:rows, :], u_pad[0 : 2 * group, :], 1, 1)
    for t in range(tiles - 1):
        p_v[t] = projected[8 * t : 8 * t + 8, :]

    pl.semaphore_wait(
        barrier,
        len(set(owners))
        + jnp.where(count > 0, 0, 1).astype(jnp.int32)
        + jnp.where(even, 5, 3).astype(jnp.int32)
        + jnp.where(heads, 1, 0).astype(jnp.int32),
    )

    signal(ready, along(lows // 2))
    signal(ready, along(-(lows // 2)))

    for t in range(tiles):

        @pl.when(plane != owners[t])
        def _():
            pltpu.make_async_remote_copy(
                src_ref=p_v.at[t],
                dst_ref=rs_v.at[slot_of[t], plane],
                send_sem=rs_send,
                recv_sem=rs_recv,
                device_id=(comp, owners[t] * highs + high),
                device_id_type=MESH,
            ).start()

    def lend(side_, core_, slot, device):
        where = set_rows(side_, core_)
        return pltpu.make_async_remote_copy(
            src_ref=u_set.at[where],
            dst_ref=u_set.at[where],
            send_sem=ux_send.at[slot],
            recv_sem=ux_recv.at[side_, core_],
            device_id=device,
            device_id_type=MESH,
        )

    def borrowed(side_, core_):
        landed(u_set.at[set_rows(side_, core_)], ux_recv.at[side_, core_])

    load_c.wait()
    lend(side, core, 0, partner).start()

    @pl.when(lends)
    def _():
        lend(side, core, 1, right).start()

    def exchange(n, device):
        return pltpu.make_async_remote_copy(
            src_ref=zs_v.at[pl.ds(0, n)],
            dst_ref=zr_v.at[side, high, pl.ds(0, n)],
            send_sem=z_send,
            recv_sem=z_recv.at[side, high],
            device_id=device,
            device_id_type=MESH,
        )

    def crossed(n, side_, high_):
        landed(zr_v.at[side_, high_, pl.ds(0, n)], z_recv.at[side_, high_])

    pl.semaphore_wait(ready, 2)
    for n in range(1, slots + 1):

        @pl.when(count == n)
        def _():
            for slot in range(n):
                rs_v[slot, plane] = p_v[first_tile + slot]
            landed(rs_v.at[pl.ds(0, n), pl.ds(0, planes - 1)], rs_recv)
            for slot in range(n):
                total = rs_v[slot, 0]
                for p in range(1, planes):
                    total = total + rs_v[slot, p]
                zs_v[slot] = total
            exchange(n, across).start()

            @pl.when(lends)
            def _():
                exchange(n, right_across).start()
                exchange(n, right).start()

            for slot in range(n):
                zr_v[side, high, slot] = zs_v[slot]

    @pl.when(heads)
    def _():
        borrowed(0, core)
        lend(0, core, 1, partner).start()

    place = core * tiles + first_tile

    def add_planes(n, side_):
        for slot in range(n):
            total = zr_v[side_, 0, slot] + zr_v[side_, 1, slot]
            tot_v[slot, side_] = total
            x_v[place + slot, side_] = total

    def spread(n, source, target):
        def spread_start(k, carry):
            @pl.when(k != itself)
            def _():
                pltpu.make_async_remote_copy(
                    src_ref=source,
                    dst_ref=target,
                    send_sem=ag_send,
                    recv_sem=ag_recv,
                    device_id=(comp, plane_at(k) * highs + high),
                    device_id_type=MESH,
                ).start()

            return carry

        lax.fori_loop(0, planes, spread_start, 0)

    for n in range(1, slots + 1):

        @pl.when(count == n)
        def _():
            crossed(n, side, 1 - high)
            add_planes(n, side)

            @pl.when(heads)
            def _():
                crossed(n, 0, 0)
                crossed(n, 0, 1)
                add_planes(n, 0)
                spread(n, tot_v.at[pl.ds(0, n)], x_v.at[pl.ds(place, n)])

            @pl.when(jnp.logical_not(heads))
            def _():
                spread(n, tot_v.at[pl.ds(0, n), side], x_v.at[pl.ds(place, n), side])

    borrowed(side, 1 - core)

    @pl.when(heads)
    def _():
        borrowed(0, 1 - core)

    def pass_on(tiles_here):
        return pltpu.make_async_remote_copy(
            src_ref=tiles_here,
            dst_ref=tiles_here,
            send_sem=xr_send,
            recv_sem=xr_recv,
            device_id=partner,
            device_id_type=MESH,
        )

    my_tiles = pl.ds(core * tiles, tiles)
    their_tiles = pl.ds((1 - core) * tiles, tiles)

    @pl.when(heads)
    def _():
        for n in range(slots + 1):

            @pl.when(count == n)
            def _():
                landed(x_v.at[pl.ds(0, tiles - n)], ag_recv)

        pass_on(x_v.at[my_tiles]).start()
        landed(x_v.at[their_tiles], xr_recv)

    @pl.when(jnp.logical_not(heads))
    def _():
        for n in range(slots + 1):

            @pl.when(count == n)
            def _():
                landed(x_v.at[pl.ds(0, tiles - n), side], ag_recv)

        pass_on(x_v.at[my_tiles, side]).start()
        landed(x_v.at[their_tiles, side], xr_recv)

    lane = lax.broadcasted_iota(jnp.int32, (8, 128), 1)
    eye = lax.broadcasted_iota(jnp.int32, (128, 128), 0) == lax.broadcasted_iota(jnp.int32, (128, 128), 1)

    def prepare(side_):
        scale0 = lax.rsqrt(x_v[tiles - 1, side_] / features + epsilon)
        scale1 = lax.rsqrt(x_v[2 * tiles - 1, side_] / features + epsilon)
        scale_row = jnp.where(lane < group, scale0, scale1)
        for t in range(tiles - 1):
            x0 = x_v[t, side_] * scale0 / root
            x1 = x_v[tiles + t, side_] * scale1 / root
            a = jnp.where(lane < group, x0, pltpu.roll(x1, 64, 1))
            b = jnp.where(lane < group, pltpu.roll(x0, 64, 1), x1)
            xt_v[side_, pl.ds(8 * t, 8), :] = a
            xt_v[side_, pl.ds(half + 8 * t, 8), :] = b
            xs_v[side_, pl.ds(8 * t, 8), :] = jnp.where(core == 0, a, b) * scale_row

    def prepare_vectors(side_):
        scale0 = lax.rsqrt(x_v[tiles - 1, side_] / features + epsilon)
        scale1 = lax.rsqrt(x_v[2 * tiles - 1, side_] / features + epsilon)
        scale_row = jnp.where(lane < group, scale0, scale1)
        scale_col = jnp.sum(
            jnp.where(eye, jnp.broadcast_to(scale_row[0:1, :], (128, 128)), 0.0), axis=1, keepdims=True
        )
        v_v[side_] = u_set[128 * side_ : 128 * side_ + 128, :] * scale_col

    @pl.when(odd)
    def _():
        prepare(1)

    @pl.when(jnp.logical_or(even, heads))
    def _():
        prepare(0)

    def add_own(b):
        columns = pl.ds(pl.multiple_of(b * 128, 128), 128)
        own_v[b] = dot(xs_v[0], u_set[0:128, columns], 1, 0)

        @pl.when(heads)
        def _():
            own_v[b] = own_v[b] + dot(xs_v[1], u_set[128:256, columns], 1, 0)

    @pl.when(jnp.logical_and(forwards, fed))
    def _():
        def each(b, carry):
            add_own(b)
            return carry

        lax.fori_loop(0, blocks, each, 0)

    my_group = pl.ds(pl.multiple_of(core * group, 8), group)

    def base():
        @pl.when(odd)
        def _():
            prepare_vectors(1)

        @pl.when(jnp.logical_or(even, heads))
        def _():
            prepare_vectors(0)

        x_own = xt_v[side]
        xtt_v[...] = x_own.T
        x_mine = xtt_v[my_group, :]
        i = lax.broadcasted_iota(jnp.int32, (group, 128), 0) + core * group
        j = lax.broadcasted_iota(jnp.int32, (group, 128), 1)
        pairs = jnp.where(j < i, dot(x_mine, x_own, 1, 0) / rows, 0.0)
        pull = dot(x_mine, s_v[...], 1, 0) * (root / rows) - dot(pairs, v_v[side], 1, 0)
        new_v[...] = v_v[side, my_group, :] + step_rate * pull

        @pl.when(heads)
        def _():
            cross = dot(x_mine, xt_v[0], 1, 0) / rows
            new_v[...] = new_v[...] - step_rate * dot(cross, v_v[0], 1, 0)

    starts = low == 1
    late = jnp.logical_and(heads, low < 5)

    @pl.when(jnp.logical_not(late))
    def _():
        base()

    def hop(b, s):
        i = b * subs + s
        here = pl.ds(pl.multiple_of(my_rows + s * sub, 8), sub)
        there = pl.ds(pl.multiple_of(s * sub, 8), sub)

        def send(src, sem, arrival, device):
            return pltpu.make_async_remote_copy(
                src_ref=src,
                dst_ref=in_v.at[b, here],
                send_sem=sem,
                recv_sem=arrival,
                device_id=device,
                device_id_type=MESH,
            )

        target = comp + jnp.where(low < lows - 3, 4, 2).astype(jnp.int32)
        forward = send(o_v.at[b, there], ch_send, ch_recv.at[i], (target, feat))
        back = send(in_v.at[b, here], lf_send, ch_recv.at[i], left)
        relay = send(in_v.at[b, here], rl_send, rl_recv.at[b], partner)
        return here, there, forward, back, relay

    def finish(b):
        other = pl.ds(pl.multiple_of((1 - core) * half, 8), half)
        landed(in_v.at[b, other], rl_recv.at[b])
        columns = pl.ds(pl.multiple_of(b * 128, 128), 128)
        new_v[:, columns] = new_v[:, columns] - dot(xtt_v[my_group, :], in_v[b], 1, 0) * (step_rate / rows)

    def chain(b, carry):
        @pl.when(starts)
        def _():
            add_own(b)

        def one(s, carry):
            here, there, forward, back, relay = hop(b, s)

            @pl.when(fed)
            def _():
                landed(in_v.at[b, here], ch_recv.at[b * subs + s])

                @pl.when(forwards)
                def _():
                    o_v[b, there] = in_v[b, here] + own_v[b, there]
                    forward.start()

                @pl.when(heads)
                def _():
                    back.start()

                relay.start()

            @pl.when(starts)
            def _():
                o_v[b, there] = own_v[b, there]
                forward.start()

            return carry

        lax.fori_loop(0, subs, one, 0)

        @pl.when(jnp.logical_and(jnp.logical_and(fed, jnp.logical_not(forwards)), b > 0))
        def _():
            finish(b - 1)

        return carry

    lax.fori_loop(0, blocks, chain, 0)

    @pl.when(jnp.logical_and(fed, jnp.logical_not(forwards)))
    def _():
        finish(blocks - 1)

    @pl.when(late)
    def _():
        base()

    @pl.when(jnp.logical_and(fed, forwards))
    def _():
        def finish_all(b, carry):
            finish(b)
            return carry

        lax.fori_loop(0, blocks, finish_all, 0)

    squares = jnp.zeros((group, 128), jnp.float32)
    for b in range(blocks):
        piece = new_v[:, b * 128 : (b + 1) * 128]
        squares = squares + piece * piece
    column = jnp.sum(squares, axis=1, keepdims=True)
    eye_half = lax.broadcasted_iota(jnp.int32, (group, 128), 0) == lax.broadcasted_iota(
        jnp.int32, (group, 128), 1
    )
    fin_v[feat] = jnp.sum(jnp.where(eye_half, column, 0.0), axis=0, keepdims=True)

    def tell(k, high_):
        pltpu.make_async_remote_copy(
            src_ref=fin_v.at[feat],
            dst_ref=fin_v.at[feat],
            send_sem=fin_send,
            recv_sem=fin_recv,
            device_id=(comp, plane_at(k) * highs + high_),
            device_id_type=MESH,
        ).start()

    def tell_across(k, carry):
        tell(k, 1 - high)
        return carry

    def tell_plane(k, carry):
        @pl.when(k != itself)
        def _():
            tell(k, high)

        return carry

    lax.fori_loop(0, planes, tell_across, 0)
    lax.fori_loop(0, planes, tell_plane, 0)
    for b in range(blocks):
        pltpu.make_async_copy(new_v.at[:, pl.ds(b * 128, 128)], out_hbm.at[b], ld_sem.at[0]).start()

    for n in range(slots + 1):

        @pl.when(count == n)
        def _():
            landed(sent_v.at[pl.ds(0, tiles - n)], rs_send)

    lend(side, core, 0, partner).wait_send()

    @pl.when(lends)
    def _():
        lend(side, core, 1, right).wait_send()

    @pl.when(heads)
    def _():
        lend(0, core, 1, partner).wait_send()

    @pl.when(heads)
    def _():
        pass_on(x_v.at[my_tiles]).wait_send()

    @pl.when(jnp.logical_not(heads))
    def _():
        pass_on(x_v.at[my_tiles, side]).wait_send()

    for n in range(1, slots + 1):

        @pl.when(count == n)
        def _():
            @pl.when(lends)
            def _():
                landed(sent_v.at[pl.ds(0, 3 * n)], z_send)

            @pl.when(jnp.logical_not(lends))
            def _():
                landed(sent_v.at[pl.ds(0, n)], z_send)

            landed(sent_v.at[pl.ds(0, n * (planes - 1))], ag_send)

            @pl.when(heads)
            def _():
                landed(sent_v.at[pl.ds(0, n * (planes - 1))], ag_send)

    @pl.when(forwards)
    def _():
        landed(o_v, ch_send)

    @pl.when(fed)
    def _():
        landed(o_v, rl_send)

        @pl.when(heads)
        def _():
            landed(o_v, lf_send)

    landed(fin_v.at[pl.ds(0, feats - 1)], fin_recv)
    total = fin_v[0]
    for q in range(1, feats):
        total = total + fin_v[q]
    scale_ref[...] = jnp.broadcast_to(
        lax.rsqrt(
            jnp.sum(jnp.where(eye_half, jnp.broadcast_to(total, (group, 128)), 0.0), axis=1, keepdims=True)
            / features
            + epsilon
        ),
        (group, 128),
    )

    landed(fin_v.at[pl.ds(0, feats - 1)], fin_send)
    landed(out_hbm, ld_sem.at[0])


def step(planes, highs, lows, sub, owners, samples, start_vectors):
    _, rows, width = samples.shape
    group = start_vectors.shape[0]
    feats = planes * highs
    half = rows // 2
    tiles = half // 8 + 1
    blocks = width // 128
    chunks = blocks * (half // sub)
    slots = max(owners.count(plane) for plane in owners)
    dma = pltpu.SemaphoreType.DMA
    f32 = jnp.float32
    updated, scale = pl.pallas_call(
        functools.partial(kernel, planes, highs, lows, sub, owners, width * feats),
        out_shape=(
            jax.ShapeDtypeStruct((blocks, group, 128), f32),
            jax.ShapeDtypeStruct((group, 128), f32),
        ),
        in_specs=[pl.BlockSpec(memory_space=pl.ANY)] * 2,
        out_specs=(pl.BlockSpec(memory_space=pl.ANY), pl.BlockSpec(memory_space=pltpu.VMEM)),
        scratch_shapes=[
            pltpu.VMEM((group, width), f32),
            pltpu.VMEM((rows, width), f32),
            pltpu.VMEM((3 * group, width), f32),
            pltpu.VMEM((4 * group, width), f32),
            pltpu.VMEM((tiles, 8, 128), f32),
            pltpu.VMEM((slots, planes, 8, 128), f32),
            pltpu.VMEM((slots, 8, 128), f32),
            pltpu.VMEM((2, 2, slots, 8, 128), f32),
            pltpu.VMEM((slots, 2, 8, 128), f32),
            pltpu.VMEM((2 * tiles, 2, 8, 128), f32),
            pltpu.VMEM((2, 2 * group, width), f32),
            pltpu.VMEM((2, rows, 128), f32),
            pltpu.VMEM((2, half, 128), f32),
            pltpu.VMEM((128, rows), f32),
            pltpu.VMEM((blocks, half, 128), f32),
            pltpu.VMEM((blocks, rows, 128), f32),
            pltpu.VMEM((blocks, half, 128), f32),
            pltpu.VMEM((feats, 1, 128), f32),
            pltpu.VMEM((slots * planes, 8, 128), f32),
            dma((4,)),
            dma((2,)),
            dma((2, 2)),
            dma,
            dma,
            dma,
            dma((2, 2)),
            dma,
            dma,
            dma,
            dma,
            dma,
            dma,
            dma((chunks,)),
            dma,
            dma((blocks,)),
            dma,
            dma,
            pltpu.SemaphoreType.REGULAR,
        ],
        compiler_params=pltpu.CompilerParams(collective_id=0, has_side_effects=True, vmem_limit_bytes=54900 * 1024),
    )(samples, start_vectors)
    return (updated * scale).transpose(1, 0, 2).reshape(group, width)


def solution(mesh, sub=SUB, owners=OWNERS, planes=16, highs=2, lows=8):
    in_specs = (P(None, None, "feat"), P("comp", "feat"))
    return jax.shard_map(
        functools.partial(step, planes, highs, lows, sub, owners),
        mesh=mesh,
        in_specs=in_specs,
        out_specs=P("comp", "feat"),
        check_vma=False,
    )
```

```python
import functools
import math

import jax
import jax.numpy as jnp
from jax import lax
from jax.experimental import pallas as pl
from jax.experimental.pallas import tpu as pltpu
from jax.sharding import PartitionSpec as P

MESH = pl.DeviceIdType.MESH
step_rate = 0.1
epsilon = 1e-06
highest = lax.Precision.HIGHEST

SUB = 24
OWNERS = (10, 10, 10, 6, 6, 6, 9, 9, 9, 11, 11, 14, 14)


def dot_exact(a, b, ca, cb):
    return lax.dot_general(
        a, b, (((ca,), (cb,)), ((), ())), precision=highest, preferred_element_type=jnp.float32
    )


def split(a):
    high = a.astype(jnp.bfloat16)
    return high, (a - high.astype(jnp.float32)).astype(jnp.bfloat16)


def dot(a, b, ca, cb):
    a_high, a_low = split(a)
    b_high, b_low = split(b)

    def product(x, y):
        return lax.dot_general(x, y, (((ca,), (cb,)), ((), ())), preferred_element_type=jnp.float32)

    return product(a_high, b_high) + (product(a_high, b_low) + product(a_low, b_high))


def landed(ref, sem):
    pltpu.make_async_copy(ref, ref, sem).wait()


def kernel(
    planes, highs, lows, sub, owners, features,
    s_hbm, u_hbm, out_hbm, scale_ref,
    new_v, s_v, u_pad, u_set, p_v, rs_v, zs_v, zr_v, tot_v, x_v, v_v, xt_v, xs_v, xtt_v, own_v, in_v, o_v, fin_v, sent_v,
    ld_sem, ux_send, ux_recv, rs_send, rs_recv, z_send, z_recv, ag_send, ag_recv, xr_send, xr_recv,
    ch_send, lf_send, ch_recv, rl_send, rl_recv, fin_send, fin_recv, ready,
):
    rows, width = s_v.shape
    half = rows // 2
    tiles = half // 8 + 1
    group = 64
    blocks = width // 128
    subs = half // sub
    feats = planes * highs
    root = math.sqrt(features)

    comp = lax.axis_index("comp")
    feat = lax.axis_index("feat")
    core = lax.rem(comp, 2)
    low = lax.div(comp, 2)
    side = lax.rem(low, 2)
    high = lax.rem(feat, highs)
    plane = lax.div(feat, highs)
    partner = (low * 2 + 1 - core, feat)
    odd = side == 1
    even = side == 0
    fed = low >= 2
    single = low >= lows - 2
    forwards = jnp.logical_or(jnp.logical_and(odd, jnp.logical_not(single)), low == lows - 2)
    lends = jnp.logical_and(even, jnp.logical_not(single))
    heads = jnp.logical_and(odd, jnp.logical_not(single))
    slot_of = [owners[:t].count(owners[t]) for t in range(tiles)]
    slots = max(slot_of) + 1
    first_tile, count = 0, 0
    for t in range(tiles):
        owned = plane == owners[t]
        count = count + jnp.where(owned, 1, 0).astype(jnp.int32)
        if slot_of[t] == 0:
            first_tile = first_tile + jnp.where(owned, t, 0).astype(jnp.int32)
    side_len = math.isqrt(planes)
    reach = side_len // 2
    here_x = lax.div(plane, side_len)
    here_y = lax.rem(plane, side_len)

    def plane_at(k):
        x = lax.rem(here_x + reach + lax.div(k, side_len), side_len)
        y = lax.rem(here_y + reach + lax.rem(k, side_len), side_len)
        return x * side_len + y

    itself = reach * side_len + reach
    my_rows = pl.multiple_of(core * half, 8)
    other_feat = plane * highs + 1 - high

    load_s = [
        pltpu.make_async_copy(s_hbm.at[0, pl.ds(r, half)], s_v.at[pl.ds(r, half)], ld_sem.at[n])
        for n, r in ((0, 0), (3, half))
    ]
    load_u = pltpu.make_async_copy(u_hbm, u_pad.at[pl.ds(group, group)], ld_sem.at[1])

    def set_rows(side_, core_):
        return pl.ds(pl.multiple_of((side_ * 2 + core_) * group, 8), group)

    own_group = set_rows(side, core)
    load_c = pltpu.make_async_copy(u_hbm, u_set.at[own_group], ld_sem.at[2])
    load_u.start()
    load_s[0].start()
    load_s[1].start()
    load_c.start()

    barrier = pltpu.get_barrier_semaphore()

    across = (comp, other_feat)
    right = (comp + 2, feat)
    right_across = (comp + 2, other_feat)
    left = (comp - 2, feat)
    ahead = (comp + 4, feat)
    behind = (comp - 4, feat)
    line = highs * lows

    def along(d):
        z = lax.rem(high * lows + low + d + line, line)
        return lax.rem(z, lows) * 2 + core, plane * highs + lax.div(z, lows)

    def signal(semaphore, device):
        pl.semaphore_signal(semaphore, inc=1, device_id=device, device_id_type=MESH)

    @pl.when(count > 0)
    def _():
        def greet(k, carry):
            @pl.when(k != itself)
            def _():
                signal(barrier, (comp, plane_at(k) * highs + high))

            return carry

        lax.fori_loop(0, planes, greet, 0)

    signal(barrier, along(lows // 2))
    signal(barrier, along(-(lows // 2)))

    @pl.when(even)
    def _():
        signal(barrier, right)

    @pl.when(odd)
    def _():
        signal(barrier, along(lows // 2 - 1))
        signal(barrier, along(-(lows // 2) - 1))
        signal(barrier, left)

        @pl.when(jnp.logical_and(fed, heads))
        def _():
            signal(barrier, behind)

    @pl.when(low == lows - 2)
    def _():
        signal(barrier, left)

    signal(barrier, partner)

    u_pad[0:group, :] = jnp.zeros((group, width), jnp.float32)
    u_pad[2 * group : 3 * group, :] = jnp.zeros((group, width), jnp.float32)
    load_u.wait()
    u_own = u_pad[group : 2 * group, :]
    squares = jnp.zeros((group, 128), jnp.float32)
    for b in range(blocks):
        piece = u_own[:, b * 128 : (b + 1) * 128]
        squares = squares + piece * piece
    squares = jnp.concatenate([squares, squares], axis=0)
    p_v[tiles - 1] = dot_exact(jnp.ones((8, 128), jnp.float32), squares, 1, 1)
    load_s[0].wait()
    projected = dot(s_v[0:half, :], u_pad[group : 3 * group, :], 1, 1)
    load_s[1].wait()
    projected = projected + dot(s_v[half:rows, :], u_pad[0 : 2 * group, :], 1, 1)
    for t in range(tiles - 1):
        p_v[t] = projected[8 * t : 8 * t + 8, :]

    pl.semaphore_wait(
        barrier,
        len(set(owners))
        + jnp.where(count > 0, 0, 1).astype(jnp.int32)
        + jnp.where(even, 5, 3).astype(jnp.int32)
        + jnp.where(heads, 1, 0).astype(jnp.int32),
    )

    signal(ready, along(lows // 2))
    signal(ready, along(-(lows // 2)))

    for t in range(tiles):

        @pl.when(plane != owners[t])
        def _():
            pltpu.make_async_remote_copy(
                src_ref=p_v.at[t],
                dst_ref=rs_v.at[slot_of[t], plane],
                send_sem=rs_send,
                recv_sem=rs_recv,
                device_id=(comp, owners[t] * highs + high),
                device_id_type=MESH,
            ).start()

    def lend(side_, core_, slot, device):
        where = set_rows(side_, core_)
        return pltpu.make_async_remote_copy(
            src_ref=u_set.at[where],
            dst_ref=u_set.at[where],
            send_sem=ux_send.at[slot],
            recv_sem=ux_recv.at[side_, core_],
            device_id=device,
            device_id_type=MESH,
        )

    def borrowed(side_, core_):
        landed(u_set.at[set_rows(side_, core_)], ux_recv.at[side_, core_])

    load_c.wait()
    lend(side, core, 0, partner).start()

    @pl.when(lends)
    def _():
        lend(side, core, 1, right).start()

    def exchange(n, device):
        return pltpu.make_async_remote_copy(
            src_ref=zs_v.at[pl.ds(0, n)],
            dst_ref=zr_v.at[side, high, pl.ds(0, n)],
            send_sem=z_send,
            recv_sem=z_recv.at[side, high],
            device_id=device,
            device_id_type=MESH,
        )

    def crossed(n, side_, high_):
        landed(zr_v.at[side_, high_, pl.ds(0, n)], z_recv.at[side_, high_])

    pl.semaphore_wait(ready, 2)
    for n in range(1, slots + 1):

        @pl.when(count == n)
        def _():
            for slot in range(n):
                rs_v[slot, plane] = p_v[first_tile + slot]
            landed(rs_v.at[pl.ds(0, n), pl.ds(0, planes - 1)], rs_recv)
            for slot in range(n):
                total = rs_v[slot, 0]
                for p in range(1, planes):
                    total = total + rs_v[slot, p]
                zs_v[slot] = total
            exchange(n, across).start()

            @pl.when(lends)
            def _():
                exchange(n, right_across).start()
                exchange(n, right).start()

            for slot in range(n):
                zr_v[side, high, slot] = zs_v[slot]

    @pl.when(heads)
    def _():
        borrowed(0, core)
        lend(0, core, 1, partner).start()

    place = core * tiles + first_tile

    def add_planes(n, side_):
        for slot in range(n):
            total = zr_v[side_, 0, slot] + zr_v[side_, 1, slot]
            tot_v[slot, side_] = total
            x_v[place + slot, side_] = total

    def spread(n, source, target):
        def spread_start(k, carry):
            @pl.when(k != itself)
            def _():
                pltpu.make_async_remote_copy(
                    src_ref=source,
                    dst_ref=target,
                    send_sem=ag_send,
                    recv_sem=ag_recv,
                    device_id=(comp, plane_at(k) * highs + high),
                    device_id_type=MESH,
                ).start()

            return carry

        lax.fori_loop(0, planes, spread_start, 0)

    for n in range(1, slots + 1):

        @pl.when(count == n)
        def _():
            crossed(n, side, 1 - high)
            add_planes(n, side)

            @pl.when(heads)
            def _():
                crossed(n, 0, 0)
                crossed(n, 0, 1)
                add_planes(n, 0)
                spread(n, tot_v.at[pl.ds(0, n)], x_v.at[pl.ds(place, n)])

            @pl.when(jnp.logical_not(heads))
            def _():
                spread(n, tot_v.at[pl.ds(0, n), side], x_v.at[pl.ds(place, n), side])

    borrowed(side, 1 - core)

    @pl.when(heads)
    def _():
        borrowed(0, 1 - core)

    def pass_on(tiles_here):
        return pltpu.make_async_remote_copy(
            src_ref=tiles_here,
            dst_ref=tiles_here,
            send_sem=xr_send,
            recv_sem=xr_recv,
            device_id=partner,
            device_id_type=MESH,
        )

    my_tiles = pl.ds(core * tiles, tiles)
    their_tiles = pl.ds((1 - core) * tiles, tiles)

    @pl.when(heads)
    def _():
        for n in range(slots + 1):

            @pl.when(count == n)
            def _():
                landed(x_v.at[pl.ds(0, tiles - n)], ag_recv)

        pass_on(x_v.at[my_tiles]).start()
        landed(x_v.at[their_tiles], xr_recv)

    @pl.when(jnp.logical_not(heads))
    def _():
        for n in range(slots + 1):

            @pl.when(count == n)
            def _():
                landed(x_v.at[pl.ds(0, tiles - n), side], ag_recv)

        pass_on(x_v.at[my_tiles, side]).start()
        landed(x_v.at[their_tiles, side], xr_recv)

    lane = lax.broadcasted_iota(jnp.int32, (8, 128), 1)
    eye = lax.broadcasted_iota(jnp.int32, (128, 128), 0) == lax.broadcasted_iota(jnp.int32, (128, 128), 1)

    def prepare(side_):
        scale0 = lax.rsqrt(x_v[tiles - 1, side_] / features + epsilon)
        scale1 = lax.rsqrt(x_v[2 * tiles - 1, side_] / features + epsilon)
        scale_row = jnp.where(lane < group, scale0, scale1)
        for t in range(tiles - 1):
            x0 = x_v[t, side_] * scale0 / root
            x1 = x_v[tiles + t, side_] * scale1 / root
            a = jnp.where(lane < group, x0, pltpu.roll(x1, 64, 1))
            b = jnp.where(lane < group, pltpu.roll(x0, 64, 1), x1)
            xt_v[side_, pl.ds(8 * t, 8), :] = a
            xt_v[side_, pl.ds(half + 8 * t, 8), :] = b
            xs_v[side_, pl.ds(8 * t, 8), :] = jnp.where(core == 0, a, b) * scale_row

    def prepare_vectors(side_):
        scale0 = lax.rsqrt(x_v[tiles - 1, side_] / features + epsilon)
        scale1 = lax.rsqrt(x_v[2 * tiles - 1, side_] / features + epsilon)
        scale_row = jnp.where(lane < group, scale0, scale1)
        scale_col = jnp.sum(
            jnp.where(eye, jnp.broadcast_to(scale_row[0:1, :], (128, 128)), 0.0), axis=1, keepdims=True
        )
        v_v[side_] = u_set[128 * side_ : 128 * side_ + 128, :] * scale_col

    @pl.when(odd)
    def _():
        prepare(1)

    @pl.when(jnp.logical_or(even, heads))
    def _():
        prepare(0)

    def add_own(b):
        columns = pl.ds(pl.multiple_of(b * 128, 128), 128)
        own_v[b] = dot(xs_v[0], u_set[0:128, columns], 1, 0)

        @pl.when(heads)
        def _():
            own_v[b] = own_v[b] + dot(xs_v[1], u_set[128:256, columns], 1, 0)

    @pl.when(jnp.logical_and(forwards, fed))
    def _():
        def each(b, carry):
            add_own(b)
            return carry

        lax.fori_loop(0, blocks, each, 0)

    my_group = pl.ds(pl.multiple_of(core * group, 8), group)

    def base():
        @pl.when(odd)
        def _():
            prepare_vectors(1)

        @pl.when(jnp.logical_or(even, heads))
        def _():
            prepare_vectors(0)

        x_own = xt_v[side]
        xtt_v[...] = x_own.T
        x_mine = xtt_v[my_group, :]
        i = lax.broadcasted_iota(jnp.int32, (group, 128), 0) + core * group
        j = lax.broadcasted_iota(jnp.int32, (group, 128), 1)
        pairs = jnp.where(j < i, dot(x_mine, x_own, 1, 0) / rows, 0.0)
        pull = dot(x_mine, s_v[...], 1, 0) * (root / rows) - dot(pairs, v_v[side], 1, 0)
        new_v[...] = v_v[side, my_group, :] + step_rate * pull

        @pl.when(heads)
        def _():
            cross = dot(x_mine, xt_v[0], 1, 0) / rows
            new_v[...] = new_v[...] - step_rate * dot(cross, v_v[0], 1, 0)

    starts = low == 1
    late = jnp.logical_and(heads, low < 5)

    @pl.when(jnp.logical_not(late))
    def _():
        base()

    def hop(b, s):
        i = b * subs + s
        here = pl.ds(pl.multiple_of(my_rows + s * sub, 8), sub)
        there = pl.ds(pl.multiple_of(s * sub, 8), sub)

        def send(src, sem, arrival, device):
            return pltpu.make_async_remote_copy(
                src_ref=src,
                dst_ref=in_v.at[b, here],
                send_sem=sem,
                recv_sem=arrival,
                device_id=device,
                device_id_type=MESH,
            )

        target = comp + jnp.where(low < lows - 3, 4, 2).astype(jnp.int32)
        forward = send(o_v.at[b, there], ch_send, ch_recv.at[i], (target, feat))
        back = send(in_v.at[b, here], lf_send, ch_recv.at[i], left)
        relay = send(in_v.at[b, here], rl_send, rl_recv.at[b], partner)
        return here, there, forward, back, relay

    def finish(b):
        other = pl.ds(pl.multiple_of((1 - core) * half, 8), half)
        landed(in_v.at[b, other], rl_recv.at[b])
        columns = pl.ds(pl.multiple_of(b * 128, 128), 128)
        new_v[:, columns] = new_v[:, columns] - dot(xtt_v[my_group, :], in_v[b], 1, 0) * (step_rate / rows)

    def chain(b, carry):
        @pl.when(starts)
        def _():
            add_own(b)

        def one(s, carry):
            here, there, forward, back, relay = hop(b, s)

            @pl.when(fed)
            def _():
                landed(in_v.at[b, here], ch_recv.at[b * subs + s])

                @pl.when(forwards)
                def _():
                    o_v[b, there] = in_v[b, here] + own_v[b, there]
                    forward.start()

                @pl.when(heads)
                def _():
                    back.start()

                relay.start()

            @pl.when(starts)
            def _():
                o_v[b, there] = own_v[b, there]
                forward.start()

            return carry

        lax.fori_loop(0, subs, one, 0)

        @pl.when(jnp.logical_and(jnp.logical_and(fed, jnp.logical_not(forwards)), b > 0))
        def _():
            finish(b - 1)

        return carry

    lax.fori_loop(0, blocks, chain, 0)

    @pl.when(jnp.logical_and(fed, jnp.logical_not(forwards)))
    def _():
        finish(blocks - 1)

    @pl.when(late)
    def _():
        base()

    @pl.when(jnp.logical_and(fed, forwards))
    def _():
        def finish_all(b, carry):
            finish(b)
            return carry

        lax.fori_loop(0, blocks, finish_all, 0)

    squares = jnp.zeros((group, 128), jnp.float32)
    for b in range(blocks):
        piece = new_v[:, b * 128 : (b + 1) * 128]
        squares = squares + piece * piece
    column = jnp.sum(squares, axis=1, keepdims=True)
    eye_half = lax.broadcasted_iota(jnp.int32, (group, 128), 0) == lax.broadcasted_iota(
        jnp.int32, (group, 128), 1
    )
    fin_v[feat] = jnp.sum(jnp.where(eye_half, column, 0.0), axis=0, keepdims=True)

    def tell(k, high_):
        pltpu.make_async_remote_copy(
            src_ref=fin_v.at[feat],
            dst_ref=fin_v.at[feat],
            send_sem=fin_send,
            recv_sem=fin_recv,
            device_id=(comp, plane_at(k) * highs + high_),
            device_id_type=MESH,
        ).start()

    def tell_across(k, carry):
        tell(k, 1 - high)
        return carry

    def tell_plane(k, carry):
        @pl.when(k != itself)
        def _():
            tell(k, high)

        return carry

    lax.fori_loop(0, planes, tell_across, 0)
    lax.fori_loop(0, planes, tell_plane, 0)
    for b in range(blocks):
        pltpu.make_async_copy(new_v.at[:, pl.ds(b * 128, 128)], out_hbm.at[b], ld_sem.at[0]).start()

    for n in range(slots + 1):

        @pl.when(count == n)
        def _():
            landed(sent_v.at[pl.ds(0, tiles - n)], rs_send)

    lend(side, core, 0, partner).wait_send()

    @pl.when(lends)
    def _():
        lend(side, core, 1, right).wait_send()

    @pl.when(heads)
    def _():
        lend(0, core, 1, partner).wait_send()

    @pl.when(heads)
    def _():
        pass_on(x_v.at[my_tiles]).wait_send()

    @pl.when(jnp.logical_not(heads))
    def _():
        pass_on(x_v.at[my_tiles, side]).wait_send()

    for n in range(1, slots + 1):

        @pl.when(count == n)
        def _():
            @pl.when(lends)
            def _():
                landed(sent_v.at[pl.ds(0, 3 * n)], z_send)

            @pl.when(jnp.logical_not(lends))
            def _():
                landed(sent_v.at[pl.ds(0, n)], z_send)

            landed(sent_v.at[pl.ds(0, n * (planes - 1))], ag_send)

            @pl.when(heads)
            def _():
                landed(sent_v.at[pl.ds(0, n * (planes - 1))], ag_send)

    @pl.when(forwards)
    def _():
        landed(o_v, ch_send)

    @pl.when(fed)
    def _():
        landed(o_v, rl_send)

        @pl.when(heads)
        def _():
            landed(o_v, lf_send)

    landed(fin_v.at[pl.ds(0, feats - 1)], fin_recv)
    total = fin_v[0]
    for q in range(1, feats):
        total = total + fin_v[q]
    scale_ref[...] = jnp.broadcast_to(
        lax.rsqrt(
            jnp.sum(jnp.where(eye_half, jnp.broadcast_to(total, (group, 128)), 0.0), axis=1, keepdims=True)
            / features
            + epsilon
        ),
        (group, 128),
    )

    landed(fin_v.at[pl.ds(0, feats - 1)], fin_send)
    landed(out_hbm, ld_sem.at[0])


def step(planes, highs, lows, sub, owners, samples, start_vectors):
    _, rows, width = samples.shape
    group = start_vectors.shape[0]
    feats = planes * highs
    half = rows // 2
    tiles = half // 8 + 1
    blocks = width // 128
    chunks = blocks * (half // sub)
    slots = max(owners.count(plane) for plane in owners)
    dma = pltpu.SemaphoreType.DMA
    f32 = jnp.float32
    updated, scale = pl.pallas_call(
        functools.partial(kernel, planes, highs, lows, sub, owners, width * feats),
        out_shape=(
            jax.ShapeDtypeStruct((blocks, group, 128), f32),
            jax.ShapeDtypeStruct((group, 128), f32),
        ),
        in_specs=[pl.BlockSpec(memory_space=pl.ANY)] * 2,
        out_specs=(pl.BlockSpec(memory_space=pl.ANY), pl.BlockSpec(memory_space=pltpu.VMEM)),
        scratch_shapes=[
            pltpu.VMEM((group, width), f32),
            pltpu.VMEM((rows, width), f32),
            pltpu.VMEM((3 * group, width), f32),
            pltpu.VMEM((4 * group, width), f32),
            pltpu.VMEM((tiles, 8, 128), f32),
            pltpu.VMEM((slots, planes, 8, 128), f32),
            pltpu.VMEM((slots, 8, 128), f32),
            pltpu.VMEM((2, 2, slots, 8, 128), f32),
            pltpu.VMEM((slots, 2, 8, 128), f32),
            pltpu.VMEM((2 * tiles, 2, 8, 128), f32),
            pltpu.VMEM((2, 2 * group, width), f32),
            pltpu.VMEM((2, rows, 128), f32),
            pltpu.VMEM((2, half, 128), f32),
            pltpu.VMEM((128, rows), f32),
            pltpu.VMEM((blocks, half, 128), f32),
            pltpu.VMEM((blocks, rows, 128), f32),
            pltpu.VMEM((blocks, half, 128), f32),
            pltpu.VMEM((feats, 1, 128), f32),
            pltpu.VMEM((slots * planes, 8, 128), f32),
            dma((4,)),
            dma((2,)),
            dma((2, 2)),
            dma,
            dma,
            dma,
            dma((2, 2)),
            dma,
            dma,
            dma,
            dma,
            dma,
            dma,
            dma((chunks,)),
            dma,
            dma((blocks,)),
            dma,
            dma,
            pltpu.SemaphoreType.REGULAR,
        ],
        compiler_params=pltpu.CompilerParams(collective_id=0, has_side_effects=True, vmem_limit_bytes=54900 * 1024),
    )(samples, start_vectors)
    return (updated * scale).transpose(1, 0, 2).reshape(group, width)


def solution(mesh, sub=SUB, owners=OWNERS, planes=16, highs=2, lows=8):
    in_specs = (P(None, None, "feat"), P("comp", "feat"))
    return jax.shard_map(
        functools.partial(step, planes, highs, lows, sub, owners),
        mesh=mesh,
        in_specs=in_specs,
        out_specs=P("comp", "feat"),
        check_vma=False,
    )
```

```python
import functools
import math

import jax
import jax.numpy as jnp
from jax import lax
from jax.experimental import pallas as pl
from jax.experimental.pallas import tpu as pltpu
from jax.sharding import PartitionSpec as P

MESH = pl.DeviceIdType.MESH
step_rate = 0.1
epsilon = 1e-06
highest = lax.Precision.HIGHEST

SUB = 24
OWNERS = (10, 10, 10, 6, 6, 6, 9, 9, 9, 11, 11, 14, 14)


def dot_exact(a, b, ca, cb):
    return lax.dot_general(
        a, b, (((ca,), (cb,)), ((), ())), precision=highest, preferred_element_type=jnp.float32
    )


def split(a):
    high = a.astype(jnp.bfloat16)
    return high, (a - high.astype(jnp.float32)).astype(jnp.bfloat16)


def dot(a, b, ca, cb):
    a_high, a_low = split(a)
    b_high, b_low = split(b)

    def product(x, y):
        return lax.dot_general(x, y, (((ca,), (cb,)), ((), ())), preferred_element_type=jnp.float32)

    return product(a_high, b_high) + (product(a_high, b_low) + product(a_low, b_high))


def landed(ref, sem):
    pltpu.make_async_copy(ref, ref, sem).wait()


def kernel(
    planes, highs, lows, sub, owners, features,
    s_hbm, u_hbm, out_hbm, scale_ref,
    new_v, s_v, u_pad, u_set, p_v, rs_v, zs_v, zr_v, tot_v, x_v, v_v, xt_v, xs_v, xtt_v, own_v, in_v, o_v, fin_v, sent_v,
    ld_sem, ux_send, ux_recv, rs_send, rs_recv, z_send, z_recv, ag_send, ag_recv, xr_send, xr_recv,
    ch_send, lf_send, ch_recv, rl_send, rl_recv, fin_send, fin_recv, ready,
):
    rows, width = s_v.shape
    half = rows // 2
    tiles = half // 8 + 1
    group = 64
    blocks = width // 128
    subs = half // sub
    feats = planes * highs
    root = math.sqrt(features)

    comp = lax.axis_index("comp")
    feat = lax.axis_index("feat")
    core = lax.rem(comp, 2)
    low = lax.div(comp, 2)
    side = lax.rem(low, 2)
    high = lax.rem(feat, highs)
    plane = lax.div(feat, highs)
    partner = (low * 2 + 1 - core, feat)
    odd = side == 1
    even = side == 0
    fed = low >= 2
    single = low >= lows - 2
    forwards = jnp.logical_or(jnp.logical_and(odd, jnp.logical_not(single)), low == lows - 2)
    lends = jnp.logical_and(even, jnp.logical_not(single))
    heads = jnp.logical_and(odd, jnp.logical_not(single))
    slot_of = [owners[:t].count(owners[t]) for t in range(tiles)]
    slots = max(slot_of) + 1
    first_tile, count = 0, 0
    for t in range(tiles):
        owned = plane == owners[t]
        count = count + jnp.where(owned, 1, 0).astype(jnp.int32)
        if slot_of[t] == 0:
            first_tile = first_tile + jnp.where(owned, t, 0).astype(jnp.int32)
    side_len = math.isqrt(planes)
    reach = side_len // 2
    here_x = lax.div(plane, side_len)
    here_y = lax.rem(plane, side_len)

    def plane_at(k):
        x = lax.rem(here_x + reach + lax.div(k, side_len), side_len)
        y = lax.rem(here_y + reach + lax.rem(k, side_len), side_len)
        return x * side_len + y

    itself = reach * side_len + reach
    my_rows = pl.multiple_of(core * half, 8)
    other_feat = plane * highs + 1 - high

    load_s = [
        pltpu.make_async_copy(s_hbm.at[0, pl.ds(r, half)], s_v.at[pl.ds(r, half)], ld_sem.at[n])
        for n, r in ((0, 0), (3, half))
    ]
    load_u = pltpu.make_async_copy(u_hbm, u_pad.at[pl.ds(group, group)], ld_sem.at[1])

    def set_rows(side_, core_):
        return pl.ds(pl.multiple_of((side_ * 2 + core_) * group, 8), group)

    own_group = set_rows(side, core)
    load_c = pltpu.make_async_copy(u_hbm, u_set.at[own_group], ld_sem.at[2])
    load_u.start()
    load_s[0].start()
    load_s[1].start()
    load_c.start()

    barrier = pltpu.get_barrier_semaphore()

    across = (comp, other_feat)
    right = (comp + 2, feat)
    right_across = (comp + 2, other_feat)
    left = (comp - 2, feat)
    ahead = (comp + 4, feat)
    behind = (comp - 4, feat)
    line = highs * lows

    def along(d):
        z = lax.rem(high * lows + low + d + line, line)
        return lax.rem(z, lows) * 2 + core, plane * highs + lax.div(z, lows)

    def signal(semaphore, device):
        pl.semaphore_signal(semaphore, inc=1, device_id=device, device_id_type=MESH)

    @pl.when(count > 0)
    def _():
        def greet(k, carry):
            @pl.when(k != itself)
            def _():
                signal(barrier, (comp, plane_at(k) * highs + high))

            return carry

        lax.fori_loop(0, planes, greet, 0)

    signal(barrier, along(lows // 2))
    signal(barrier, along(-(lows // 2)))

    @pl.when(even)
    def _():
        signal(barrier, right)

    @pl.when(odd)
    def _():
        signal(barrier, along(lows // 2 - 1))
        signal(barrier, along(-(lows // 2) - 1))
        signal(barrier, left)

        @pl.when(jnp.logical_and(fed, heads))
        def _():
            signal(barrier, behind)

    @pl.when(low == lows - 2)
    def _():
        signal(barrier, left)

    signal(barrier, partner)

    u_pad[0:group, :] = jnp.zeros((group, width), jnp.float32)
    u_pad[2 * group : 3 * group, :] = jnp.zeros((group, width), jnp.float32)
    load_u.wait()
    u_own = u_pad[group : 2 * group, :]
    squares = jnp.zeros((group, 128), jnp.float32)
    for b in range(blocks):
        piece = u_own[:, b * 128 : (b + 1) * 128]
        squares = squares + piece * piece
    squares = jnp.concatenate([squares, squares], axis=0)
    p_v[tiles - 1] = dot_exact(jnp.ones((8, 128), jnp.float32), squares, 1, 1)
    load_s[0].wait()
    projected = dot(s_v[0:half, :], u_pad[group : 3 * group, :], 1, 1)
    load_s[1].wait()
    projected = projected + dot(s_v[half:rows, :], u_pad[0 : 2 * group, :], 1, 1)
    for t in range(tiles - 1):
        p_v[t] = projected[8 * t : 8 * t + 8, :]

    pl.semaphore_wait(
        barrier,
        len(set(owners))
        + jnp.where(count > 0, 0, 1).astype(jnp.int32)
        + jnp.where(even, 5, 3).astype(jnp.int32)
        + jnp.where(heads, 1, 0).astype(jnp.int32),
    )

    signal(ready, along(lows // 2))
    signal(ready, along(-(lows // 2)))

    for t in range(tiles):

        @pl.when(plane != owners[t])
        def _():
            pltpu.make_async_remote_copy(
                src_ref=p_v.at[t],
                dst_ref=rs_v.at[slot_of[t], plane],
                send_sem=rs_send,
                recv_sem=rs_recv,
                device_id=(comp, owners[t] * highs + high),
                device_id_type=MESH,
            ).start()

    def lend(side_, core_, slot, device):
        where = set_rows(side_, core_)
        return pltpu.make_async_remote_copy(
            src_ref=u_set.at[where],
            dst_ref=u_set.at[where],
            send_sem=ux_send.at[slot],
            recv_sem=ux_recv.at[side_, core_],
            device_id=device,
            device_id_type=MESH,
        )

    def borrowed(side_, core_):
        landed(u_set.at[set_rows(side_, core_)], ux_recv.at[side_, core_])

    load_c.wait()
    lend(side, core, 0, partner).start()

    @pl.when(lends)
    def _():
        lend(side, core, 1, right).start()

    def exchange(n, device):
        return pltpu.make_async_remote_copy(
            src_ref=zs_v.at[pl.ds(0, n)],
            dst_ref=zr_v.at[side, high, pl.ds(0, n)],
            send_sem=z_send,
            recv_sem=z_recv.at[side, high],
            device_id=device,
            device_id_type=MESH,
        )

    def crossed(n, side_, high_):
        landed(zr_v.at[side_, high_, pl.ds(0, n)], z_recv.at[side_, high_])

    @pl.when(count == 0)
    def _():
        pl.semaphore_wait(ready, 2)

    for n in range(1, slots + 1):

        @pl.when(count == n)
        def _():
            for slot in range(n):
                rs_v[slot, plane] = p_v[first_tile + slot]
            landed(rs_v.at[pl.ds(0, n), pl.ds(0, planes - 1)], rs_recv)
            for slot in range(n):
                total = rs_v[slot, 0]
                for p in range(1, planes):
                    total = total + rs_v[slot, p]
                zs_v[slot] = total
            pl.semaphore_wait(ready, 2)
            exchange(n, across).start()

            @pl.when(lends)
            def _():
                exchange(n, right_across).start()
                exchange(n, right).start()

            for slot in range(n):
                zr_v[side, high, slot] = zs_v[slot]

    @pl.when(heads)
    def _():
        borrowed(0, core)
        lend(0, core, 1, partner).start()

    place = core * tiles + first_tile

    def add_planes(n, side_):
        for slot in range(n):
            total = zr_v[side_, 0, slot] + zr_v[side_, 1, slot]
            tot_v[slot, side_] = total
            x_v[place + slot, side_] = total

    def spread(n, source, target):
        def spread_start(k, carry):
            @pl.when(k != itself)
            def _():
                pltpu.make_async_remote_copy(
                    src_ref=source,
                    dst_ref=target,
                    send_sem=ag_send,
                    recv_sem=ag_recv,
                    device_id=(comp, plane_at(k) * highs + high),
                    device_id_type=MESH,
                ).start()

            return carry

        lax.fori_loop(0, planes, spread_start, 0)

    for n in range(1, slots + 1):

        @pl.when(count == n)
        def _():
            crossed(n, side, 1 - high)
            add_planes(n, side)

            @pl.when(heads)
            def _():
                crossed(n, 0, 0)
                crossed(n, 0, 1)
                add_planes(n, 0)
                spread(n, tot_v.at[pl.ds(0, n)], x_v.at[pl.ds(place, n)])

            @pl.when(jnp.logical_not(heads))
            def _():
                spread(n, tot_v.at[pl.ds(0, n), side], x_v.at[pl.ds(place, n), side])

    borrowed(side, 1 - core)

    @pl.when(heads)
    def _():
        borrowed(0, 1 - core)

    def pass_on(tiles_here):
        return pltpu.make_async_remote_copy(
            src_ref=tiles_here,
            dst_ref=tiles_here,
            send_sem=xr_send,
            recv_sem=xr_recv,
            device_id=partner,
            device_id_type=MESH,
        )

    my_tiles = pl.ds(core * tiles, tiles)
    their_tiles = pl.ds((1 - core) * tiles, tiles)

    @pl.when(heads)
    def _():
        for n in range(slots + 1):

            @pl.when(count == n)
            def _():
                landed(x_v.at[pl.ds(0, tiles - n)], ag_recv)

        pass_on(x_v.at[my_tiles]).start()
        landed(x_v.at[their_tiles], xr_recv)

    @pl.when(jnp.logical_not(heads))
    def _():
        for n in range(slots + 1):

            @pl.when(count == n)
            def _():
                landed(x_v.at[pl.ds(0, tiles - n), side], ag_recv)

        pass_on(x_v.at[my_tiles, side]).start()
        landed(x_v.at[their_tiles, side], xr_recv)

    lane = lax.broadcasted_iota(jnp.int32, (8, 128), 1)
    eye = lax.broadcasted_iota(jnp.int32, (128, 128), 0) == lax.broadcasted_iota(jnp.int32, (128, 128), 1)

    def prepare(side_):
        scale0 = lax.rsqrt(x_v[tiles - 1, side_] / features + epsilon)
        scale1 = lax.rsqrt(x_v[2 * tiles - 1, side_] / features + epsilon)
        scale_row = jnp.where(lane < group, scale0, scale1)
        for t in range(tiles - 1):
            x0 = x_v[t, side_] * scale0 / root
            x1 = x_v[tiles + t, side_] * scale1 / root
            a = jnp.where(lane < group, x0, pltpu.roll(x1, 64, 1))
            b = jnp.where(lane < group, pltpu.roll(x0, 64, 1), x1)
            xt_v[side_, pl.ds(8 * t, 8), :] = a
            xt_v[side_, pl.ds(half + 8 * t, 8), :] = b
            xs_v[side_, pl.ds(8 * t, 8), :] = jnp.where(core == 0, a, b) * scale_row

    def prepare_vectors(side_):
        scale0 = lax.rsqrt(x_v[tiles - 1, side_] / features + epsilon)
        scale1 = lax.rsqrt(x_v[2 * tiles - 1, side_] / features + epsilon)
        scale_row = jnp.where(lane < group, scale0, scale1)
        scale_col = jnp.sum(
            jnp.where(eye, jnp.broadcast_to(scale_row[0:1, :], (128, 128)), 0.0), axis=1, keepdims=True
        )
        v_v[side_] = u_set[128 * side_ : 128 * side_ + 128, :] * scale_col

    @pl.when(odd)
    def _():
        prepare(1)

    @pl.when(jnp.logical_or(even, heads))
    def _():
        prepare(0)

    def add_own(b):
        columns = pl.ds(pl.multiple_of(b * 128, 128), 128)
        own_v[b] = dot(xs_v[0], u_set[0:128, columns], 1, 0)

        @pl.when(heads)
        def _():
            own_v[b] = own_v[b] + dot(xs_v[1], u_set[128:256, columns], 1, 0)

    @pl.when(jnp.logical_and(forwards, fed))
    def _():
        def each(b, carry):
            add_own(b)
            return carry

        lax.fori_loop(0, blocks, each, 0)

    my_group = pl.ds(pl.multiple_of(core * group, 8), group)

    def base():
        @pl.when(odd)
        def _():
            prepare_vectors(1)

        @pl.when(jnp.logical_or(even, heads))
        def _():
            prepare_vectors(0)

        x_own = xt_v[side]
        xtt_v[...] = x_own.T
        x_mine = xtt_v[my_group, :]
        i = lax.broadcasted_iota(jnp.int32, (group, 128), 0) + core * group
        j = lax.broadcasted_iota(jnp.int32, (group, 128), 1)
        pairs = jnp.where(j < i, dot(x_mine, x_own, 1, 0) / rows, 0.0)
        pull = dot(x_mine, s_v[...], 1, 0) * (root / rows) - dot(pairs, v_v[side], 1, 0)
        new_v[...] = v_v[side, my_group, :] + step_rate * pull

        @pl.when(heads)
        def _():
            cross = dot(x_mine, xt_v[0], 1, 0) / rows
            new_v[...] = new_v[...] - step_rate * dot(cross, v_v[0], 1, 0)

    starts = low == 1
    late = jnp.logical_and(heads, low < 5)

    @pl.when(jnp.logical_not(late))
    def _():
        base()

    def hop(b, s):
        i = b * subs + s
        here = pl.ds(pl.multiple_of(my_rows + s * sub, 8), sub)
        there = pl.ds(pl.multiple_of(s * sub, 8), sub)

        def send(src, sem, arrival, device):
            return pltpu.make_async_remote_copy(
                src_ref=src,
                dst_ref=in_v.at[b, here],
                send_sem=sem,
                recv_sem=arrival,
                device_id=device,
                device_id_type=MESH,
            )

        target = comp + jnp.where(low < lows - 3, 4, 2).astype(jnp.int32)
        forward = send(o_v.at[b, there], ch_send, ch_recv.at[i], (target, feat))
        back = send(in_v.at[b, here], lf_send, ch_recv.at[i], left)
        relay = send(in_v.at[b, here], rl_send, rl_recv.at[b], partner)
        return here, there, forward, back, relay

    def finish(b):
        other = pl.ds(pl.multiple_of((1 - core) * half, 8), half)
        landed(in_v.at[b, other], rl_recv.at[b])
        columns = pl.ds(pl.multiple_of(b * 128, 128), 128)
        new_v[:, columns] = new_v[:, columns] - dot(xtt_v[my_group, :], in_v[b], 1, 0) * (step_rate / rows)

    def chain(b, carry):
        @pl.when(starts)
        def _():
            add_own(b)

        def one(s, carry):
            here, there, forward, back, relay = hop(b, s)

            @pl.when(fed)
            def _():
                landed(in_v.at[b, here], ch_recv.at[b * subs + s])

                @pl.when(forwards)
                def _():
                    o_v[b, there] = in_v[b, here] + own_v[b, there]
                    forward.start()

                @pl.when(heads)
                def _():
                    back.start()

                relay.start()

            @pl.when(starts)
            def _():
                o_v[b, there] = own_v[b, there]
                forward.start()

            return carry

        lax.fori_loop(0, subs, one, 0)

        @pl.when(jnp.logical_and(jnp.logical_and(fed, jnp.logical_not(forwards)), b > 0))
        def _():
            finish(b - 1)

        return carry

    lax.fori_loop(0, blocks, chain, 0)

    @pl.when(jnp.logical_and(fed, jnp.logical_not(forwards)))
    def _():
        finish(blocks - 1)

    @pl.when(late)
    def _():
        base()

    @pl.when(jnp.logical_and(fed, forwards))
    def _():
        def finish_all(b, carry):
            finish(b)
            return carry

        lax.fori_loop(0, blocks, finish_all, 0)

    squares = jnp.zeros((group, 128), jnp.float32)
    for b in range(blocks):
        piece = new_v[:, b * 128 : (b + 1) * 128]
        squares = squares + piece * piece
    column = jnp.sum(squares, axis=1, keepdims=True)
    eye_half = lax.broadcasted_iota(jnp.int32, (group, 128), 0) == lax.broadcasted_iota(
        jnp.int32, (group, 128), 1
    )
    fin_v[feat] = jnp.sum(jnp.where(eye_half, column, 0.0), axis=0, keepdims=True)

    def tell(k, high_):
        pltpu.make_async_remote_copy(
            src_ref=fin_v.at[feat],
            dst_ref=fin_v.at[feat],
            send_sem=fin_send,
            recv_sem=fin_recv,
            device_id=(comp, plane_at(k) * highs + high_),
            device_id_type=MESH,
        ).start()

    def tell_across(k, carry):
        tell(k, 1 - high)
        return carry

    def tell_plane(k, carry):
        @pl.when(k != itself)
        def _():
            tell(k, high)

        return carry

    lax.fori_loop(0, planes, tell_across, 0)
    lax.fori_loop(0, planes, tell_plane, 0)
    for b in range(blocks):
        pltpu.make_async_copy(new_v.at[:, pl.ds(b * 128, 128)], out_hbm.at[b], ld_sem.at[0]).start()

    for n in range(slots + 1):

        @pl.when(count == n)
        def _():
            landed(sent_v.at[pl.ds(0, tiles - n)], rs_send)

    lend(side, core, 0, partner).wait_send()

    @pl.when(lends)
    def _():
        lend(side, core, 1, right).wait_send()

    @pl.when(heads)
    def _():
        lend(0, core, 1, partner).wait_send()

    @pl.when(heads)
    def _():
        pass_on(x_v.at[my_tiles]).wait_send()

    @pl.when(jnp.logical_not(heads))
    def _():
        pass_on(x_v.at[my_tiles, side]).wait_send()

    for n in range(1, slots + 1):

        @pl.when(count == n)
        def _():
            @pl.when(lends)
            def _():
                landed(sent_v.at[pl.ds(0, 3 * n)], z_send)

            @pl.when(jnp.logical_not(lends))
            def _():
                landed(sent_v.at[pl.ds(0, n)], z_send)

            landed(sent_v.at[pl.ds(0, n * (planes - 1))], ag_send)

            @pl.when(heads)
            def _():
                landed(sent_v.at[pl.ds(0, n * (planes - 1))], ag_send)

    @pl.when(forwards)
    def _():
        landed(o_v, ch_send)

    @pl.when(fed)
    def _():
        landed(o_v, rl_send)

        @pl.when(heads)
        def _():
            landed(o_v, lf_send)

    landed(fin_v.at[pl.ds(0, feats - 1)], fin_recv)
    total = fin_v[0]
    for q in range(1, feats):
        total = total + fin_v[q]
    scale_ref[...] = jnp.broadcast_to(
        lax.rsqrt(
            jnp.sum(jnp.where(eye_half, jnp.broadcast_to(total, (group, 128)), 0.0), axis=1, keepdims=True)
            / features
            + epsilon
        ),
        (group, 128),
    )

    landed(fin_v.at[pl.ds(0, feats - 1)], fin_send)
    landed(out_hbm, ld_sem.at[0])


def step(planes, highs, lows, sub, owners, samples, start_vectors):
    _, rows, width = samples.shape
    group = start_vectors.shape[0]
    feats = planes * highs
    half = rows // 2
    tiles = half // 8 + 1
    blocks = width // 128
    chunks = blocks * (half // sub)
    slots = max(owners.count(plane) for plane in owners)
    dma = pltpu.SemaphoreType.DMA
    f32 = jnp.float32
    updated, scale = pl.pallas_call(
        functools.partial(kernel, planes, highs, lows, sub, owners, width * feats),
        out_shape=(
            jax.ShapeDtypeStruct((blocks, group, 128), f32),
            jax.ShapeDtypeStruct((group, 128), f32),
        ),
        in_specs=[pl.BlockSpec(memory_space=pl.ANY)] * 2,
        out_specs=(pl.BlockSpec(memory_space=pl.ANY), pl.BlockSpec(memory_space=pltpu.VMEM)),
        scratch_shapes=[
            pltpu.VMEM((group, width), f32),
            pltpu.VMEM((rows, width), f32),
            pltpu.VMEM((3 * group, width), f32),
            pltpu.VMEM((4 * group, width), f32),
            pltpu.VMEM((tiles, 8, 128), f32),
            pltpu.VMEM((slots, planes, 8, 128), f32),
            pltpu.VMEM((slots, 8, 128), f32),
            pltpu.VMEM((2, 2, slots, 8, 128), f32),
            pltpu.VMEM((slots, 2, 8, 128), f32),
            pltpu.VMEM((2 * tiles, 2, 8, 128), f32),
            pltpu.VMEM((2, 2 * group, width), f32),
            pltpu.VMEM((2, rows, 128), f32),
            pltpu.VMEM((2, half, 128), f32),
            pltpu.VMEM((128, rows), f32),
            pltpu.VMEM((blocks, half, 128), f32),
            pltpu.VMEM((blocks, rows, 128), f32),
            pltpu.VMEM((blocks, half, 128), f32),
            pltpu.VMEM((feats, 1, 128), f32),
            pltpu.VMEM((slots * planes, 8, 128), f32),
            dma((4,)),
            dma((2,)),
            dma((2, 2)),
            dma,
            dma,
            dma,
            dma((2, 2)),
            dma,
            dma,
            dma,
            dma,
            dma,
            dma,
            dma((chunks,)),
            dma,
            dma((blocks,)),
            dma,
            dma,
            pltpu.SemaphoreType.REGULAR,
        ],
        compiler_params=pltpu.CompilerParams(collective_id=0, has_side_effects=True, vmem_limit_bytes=54900 * 1024),
    )(samples, start_vectors)
    return (updated * scale).transpose(1, 0, 2).reshape(group, width)


def solution(mesh, sub=SUB, owners=OWNERS, planes=16, highs=2, lows=8):
    in_specs = (P(None, None, "feat"), P("comp", "feat"))
    return jax.shard_map(
        functools.partial(step, planes, highs, lows, sub, owners),
        mesh=mesh,
        in_specs=in_specs,
        out_specs=P("comp", "feat"),
        check_vma=False,
    )
```

```python
import functools
import math

import jax
import jax.numpy as jnp
from jax import lax
from jax.experimental import pallas as pl
from jax.experimental.pallas import tpu as pltpu
from jax.sharding import PartitionSpec as P

MESH = pl.DeviceIdType.MESH
step_rate = 0.1
epsilon = 1e-06
highest = lax.Precision.HIGHEST

SUB = 24
OWNERS = (10, 10, 10, 6, 6, 6, 9, 9, 9, 11, 11, 14, 14)


def dot_exact(a, b, ca, cb):
    return lax.dot_general(
        a, b, (((ca,), (cb,)), ((), ())), precision=highest, preferred_element_type=jnp.float32
    )


def split(a):
    high = a.astype(jnp.bfloat16)
    return high, (a - high.astype(jnp.float32)).astype(jnp.bfloat16)


def dot(a, b, ca, cb):
    a_high, a_low = split(a)
    b_high, b_low = split(b)

    def product(x, y):
        return lax.dot_general(x, y, (((ca,), (cb,)), ((), ())), preferred_element_type=jnp.float32)

    return product(a_high, b_high) + (product(a_high, b_low) + product(a_low, b_high))


def landed(ref, sem):
    pltpu.make_async_copy(ref, ref, sem).wait()


def kernel(
    planes, highs, lows, sub, owners, features,
    s_hbm, u_hbm, out_hbm, scale_ref,
    new_v, s_v, u_pad, u_set, p_v, rs_v, zs_v, zr_v, tot_v, x_v, v_v, xt_v, xs_v, xtt_v, own_v, in_v, o_v, fin_v, sent_v,
    ld_sem, ux_send, ux_recv, rs_send, rs_recv, z_send, z_recv, ag_send, ag_recv, xr_send, xr_recv,
    ch_send, lf_send, ch_recv, rl_send, rl_recv, fin_send, fin_recv, ready,
):
    rows, width = s_v.shape
    half = rows // 2
    tiles = half // 8 + 1
    group = 64
    blocks = width // 128
    subs = half // sub
    feats = planes * highs
    root = math.sqrt(features)

    comp = lax.axis_index("comp")
    feat = lax.axis_index("feat")
    core = lax.rem(comp, 2)
    low = lax.div(comp, 2)
    side = lax.rem(low, 2)
    high = lax.rem(feat, highs)
    plane = lax.div(feat, highs)
    partner = (low * 2 + 1 - core, feat)
    odd = side == 1
    even = side == 0
    fed = low >= 2
    single = low >= lows - 2
    forwards = jnp.logical_or(jnp.logical_and(odd, jnp.logical_not(single)), low == lows - 2)
    lends = jnp.logical_and(even, jnp.logical_not(single))
    heads = jnp.logical_and(odd, jnp.logical_not(single))
    slot_of = [owners[:t].count(owners[t]) for t in range(tiles)]
    slots = max(slot_of) + 1
    first_tile, count = 0, 0
    for t in range(tiles):
        owned = plane == owners[t]
        count = count + jnp.where(owned, 1, 0).astype(jnp.int32)
        if slot_of[t] == 0:
            first_tile = first_tile + jnp.where(owned, t, 0).astype(jnp.int32)
    side_len = math.isqrt(planes)
    reach = side_len // 2
    here_x = lax.div(plane, side_len)
    here_y = lax.rem(plane, side_len)

    def plane_at(k):
        x = lax.rem(here_x + reach + lax.div(k, side_len), side_len)
        y = lax.rem(here_y + reach + lax.rem(k, side_len), side_len)
        return x * side_len + y

    itself = reach * side_len + reach
    my_rows = pl.multiple_of(core * half, 8)
    other_feat = plane * highs + 1 - high

    load_s = [
        pltpu.make_async_copy(s_hbm.at[0, pl.ds(r, half)], s_v.at[pl.ds(r, half)], ld_sem.at[n])
        for n, r in ((0, 0), (3, half))
    ]
    load_u = pltpu.make_async_copy(u_hbm, u_pad.at[pl.ds(group, group)], ld_sem.at[1])

    def set_rows(side_, core_):
        return pl.ds(pl.multiple_of((side_ * 2 + core_) * group, 8), group)

    own_group = set_rows(side, core)
    load_c = pltpu.make_async_copy(u_hbm, u_set.at[own_group], ld_sem.at[2])
    load_u.start()
    load_s[0].start()
    load_s[1].start()
    load_c.start()

    barrier = pltpu.get_barrier_semaphore()

    across = (comp, other_feat)
    right = (comp + 2, feat)
    right_across = (comp + 2, other_feat)
    left = (comp - 2, feat)
    ahead = (comp + 4, feat)
    behind = (comp - 4, feat)
    line = highs * lows

    def along(d):
        z = lax.rem(high * lows + low + d + line, line)
        return lax.rem(z, lows) * 2 + core, plane * highs + lax.div(z, lows)

    def signal(semaphore, device):
        pl.semaphore_signal(semaphore, inc=1, device_id=device, device_id_type=MESH)

    signal(barrier, along(lows // 2))
    signal(barrier, along(-(lows // 2)))

    @pl.when(count > 0)
    def _():
        def greet(k, carry):
            @pl.when(k != itself)
            def _():
                signal(barrier, (comp, plane_at(k) * highs + high))

            return carry

        lax.fori_loop(0, planes, greet, 0)

    @pl.when(even)
    def _():
        signal(barrier, right)

    @pl.when(odd)
    def _():
        signal(barrier, along(lows // 2 - 1))
        signal(barrier, along(-(lows // 2) - 1))
        signal(barrier, left)

        @pl.when(jnp.logical_and(fed, heads))
        def _():
            signal(barrier, behind)

    @pl.when(low == lows - 2)
    def _():
        signal(barrier, left)

    signal(barrier, partner)

    u_pad[0:group, :] = jnp.zeros((group, width), jnp.float32)
    u_pad[2 * group : 3 * group, :] = jnp.zeros((group, width), jnp.float32)
    load_u.wait()
    u_own = u_pad[group : 2 * group, :]
    squares = jnp.zeros((group, 128), jnp.float32)
    for b in range(blocks):
        piece = u_own[:, b * 128 : (b + 1) * 128]
        squares = squares + piece * piece
    squares = jnp.concatenate([squares, squares], axis=0)
    p_v[tiles - 1] = dot_exact(jnp.ones((8, 128), jnp.float32), squares, 1, 1)
    load_s[0].wait()
    projected = dot(s_v[0:half, :], u_pad[group : 3 * group, :], 1, 1)
    load_s[1].wait()
    projected = projected + dot(s_v[half:rows, :], u_pad[0 : 2 * group, :], 1, 1)
    for t in range(tiles - 1):
        p_v[t] = projected[8 * t : 8 * t + 8, :]

    pl.semaphore_wait(
        barrier,
        len(set(owners))
        + jnp.where(count > 0, 0, 1).astype(jnp.int32)
        + jnp.where(even, 5, 3).astype(jnp.int32)
        + jnp.where(heads, 1, 0).astype(jnp.int32),
    )

    signal(ready, along(lows // 2))
    signal(ready, along(-(lows // 2)))

    for t in range(tiles):

        @pl.when(plane != owners[t])
        def _():
            pltpu.make_async_remote_copy(
                src_ref=p_v.at[t],
                dst_ref=rs_v.at[slot_of[t], plane],
                send_sem=rs_send,
                recv_sem=rs_recv,
                device_id=(comp, owners[t] * highs + high),
                device_id_type=MESH,
            ).start()

    def lend(side_, core_, slot, device):
        where = set_rows(side_, core_)
        return pltpu.make_async_remote_copy(
            src_ref=u_set.at[where],
            dst_ref=u_set.at[where],
            send_sem=ux_send.at[slot],
            recv_sem=ux_recv.at[side_, core_],
            device_id=device,
            device_id_type=MESH,
        )

    def borrowed(side_, core_):
        landed(u_set.at[set_rows(side_, core_)], ux_recv.at[side_, core_])

    load_c.wait()
    lend(side, core, 0, partner).start()

    @pl.when(lends)
    def _():
        lend(side, core, 1, right).start()

    def exchange(n, device):
        return pltpu.make_async_remote_copy(
            src_ref=zs_v.at[pl.ds(0, n)],
            dst_ref=zr_v.at[side, high, pl.ds(0, n)],
            send_sem=z_send,
            recv_sem=z_recv.at[side, high],
            device_id=device,
            device_id_type=MESH,
        )

    def crossed(n, side_, high_):
        landed(zr_v.at[side_, high_, pl.ds(0, n)], z_recv.at[side_, high_])

    @pl.when(count == 0)
    def _():
        pl.semaphore_wait(ready, 2)

    for n in range(1, slots + 1):

        @pl.when(count == n)
        def _():
            for slot in range(n):
                rs_v[slot, plane] = p_v[first_tile + slot]
            landed(rs_v.at[pl.ds(0, n), pl.ds(0, planes - 1)], rs_recv)
            for slot in range(n):
                total = rs_v[slot, 0]
                for p in range(1, planes):
                    total = total + rs_v[slot, p]
                zs_v[slot] = total
            pl.semaphore_wait(ready, 2)
            exchange(n, across).start()

            @pl.when(lends)
            def _():
                exchange(n, right_across).start()
                exchange(n, right).start()

            for slot in range(n):
                zr_v[side, high, slot] = zs_v[slot]

    @pl.when(heads)
    def _():
        borrowed(0, core)
        lend(0, core, 1, partner).start()

    place = core * tiles + first_tile

    def add_planes(n, side_):
        for slot in range(n):
            total = zr_v[side_, 0, slot] + zr_v[side_, 1, slot]
            tot_v[slot, side_] = total
            x_v[place + slot, side_] = total

    def spread(n, source, target):
        def spread_start(k, carry):
            @pl.when(k != itself)
            def _():
                pltpu.make_async_remote_copy(
                    src_ref=source,
                    dst_ref=target,
                    send_sem=ag_send,
                    recv_sem=ag_recv,
                    device_id=(comp, plane_at(k) * highs + high),
                    device_id_type=MESH,
                ).start()

            return carry

        lax.fori_loop(0, planes, spread_start, 0)

    for n in range(1, slots + 1):

        @pl.when(count == n)
        def _():
            crossed(n, side, 1 - high)
            add_planes(n, side)

            @pl.when(heads)
            def _():
                crossed(n, 0, 0)
                crossed(n, 0, 1)
                add_planes(n, 0)
                spread(n, tot_v.at[pl.ds(0, n)], x_v.at[pl.ds(place, n)])

            @pl.when(jnp.logical_not(heads))
            def _():
                spread(n, tot_v.at[pl.ds(0, n), side], x_v.at[pl.ds(place, n), side])

    borrowed(side, 1 - core)

    @pl.when(heads)
    def _():
        borrowed(0, 1 - core)

    def pass_on(tiles_here):
        return pltpu.make_async_remote_copy(
            src_ref=tiles_here,
            dst_ref=tiles_here,
            send_sem=xr_send,
            recv_sem=xr_recv,
            device_id=partner,
            device_id_type=MESH,
        )

    my_tiles = pl.ds(core * tiles, tiles)
    their_tiles = pl.ds((1 - core) * tiles, tiles)

    @pl.when(heads)
    def _():
        for n in range(slots + 1):

            @pl.when(count == n)
            def _():
                landed(x_v.at[pl.ds(0, tiles - n)], ag_recv)

        pass_on(x_v.at[my_tiles]).start()
        landed(x_v.at[their_tiles], xr_recv)

    @pl.when(jnp.logical_not(heads))
    def _():
        for n in range(slots + 1):

            @pl.when(count == n)
            def _():
                landed(x_v.at[pl.ds(0, tiles - n), side], ag_recv)

        pass_on(x_v.at[my_tiles, side]).start()
        landed(x_v.at[their_tiles, side], xr_recv)

    lane = lax.broadcasted_iota(jnp.int32, (8, 128), 1)
    eye = lax.broadcasted_iota(jnp.int32, (128, 128), 0) == lax.broadcasted_iota(jnp.int32, (128, 128), 1)

    def prepare(side_):
        scale0 = lax.rsqrt(x_v[tiles - 1, side_] / features + epsilon)
        scale1 = lax.rsqrt(x_v[2 * tiles - 1, side_] / features + epsilon)
        scale_row = jnp.where(lane < group, scale0, scale1)
        for t in range(tiles - 1):
            x0 = x_v[t, side_] * scale0 / root
            x1 = x_v[tiles + t, side_] * scale1 / root
            a = jnp.where(lane < group, x0, pltpu.roll(x1, 64, 1))
            b = jnp.where(lane < group, pltpu.roll(x0, 64, 1), x1)
            xt_v[side_, pl.ds(8 * t, 8), :] = a
            xt_v[side_, pl.ds(half + 8 * t, 8), :] = b
            xs_v[side_, pl.ds(8 * t, 8), :] = jnp.where(core == 0, a, b) * scale_row

    def prepare_vectors(side_):
        scale0 = lax.rsqrt(x_v[tiles - 1, side_] / features + epsilon)
        scale1 = lax.rsqrt(x_v[2 * tiles - 1, side_] / features + epsilon)
        scale_row = jnp.where(lane < group, scale0, scale1)
        scale_col = jnp.sum(
            jnp.where(eye, jnp.broadcast_to(scale_row[0:1, :], (128, 128)), 0.0), axis=1, keepdims=True
        )
        v_v[side_] = u_set[128 * side_ : 128 * side_ + 128, :] * scale_col

    @pl.when(odd)
    def _():
        prepare(1)

    @pl.when(jnp.logical_or(even, heads))
    def _():
        prepare(0)

    def add_own(b):
        columns = pl.ds(pl.multiple_of(b * 128, 128), 128)
        own_v[b] = dot(xs_v[0], u_set[0:128, columns], 1, 0)

        @pl.when(heads)
        def _():
            own_v[b] = own_v[b] + dot(xs_v[1], u_set[128:256, columns], 1, 0)

    @pl.when(jnp.logical_and(forwards, fed))
    def _():
        def each(b, carry):
            add_own(b)
            return carry

        lax.fori_loop(0, blocks, each, 0)

    my_group = pl.ds(pl.multiple_of(core * group, 8), group)

    def base():
        @pl.when(odd)
        def _():
            prepare_vectors(1)

        @pl.when(jnp.logical_or(even, heads))
        def _():
            prepare_vectors(0)

        x_own = xt_v[side]
        xtt_v[...] = x_own.T
        x_mine = xtt_v[my_group, :]
        i = lax.broadcasted_iota(jnp.int32, (group, 128), 0) + core * group
        j = lax.broadcasted_iota(jnp.int32, (group, 128), 1)
        pairs = jnp.where(j < i, dot(x_mine, x_own, 1, 0) / rows, 0.0)
        pull = dot(x_mine, s_v[...], 1, 0) * (root / rows) - dot(pairs, v_v[side], 1, 0)
        new_v[...] = v_v[side, my_group, :] + step_rate * pull

        @pl.when(heads)
        def _():
            cross = dot(x_mine, xt_v[0], 1, 0) / rows
            new_v[...] = new_v[...] - step_rate * dot(cross, v_v[0], 1, 0)

    starts = low == 1
    late = jnp.logical_and(heads, low < 5)

    @pl.when(jnp.logical_not(late))
    def _():
        base()

    def hop(b, s):
        i = b * subs + s
        here = pl.ds(pl.multiple_of(my_rows + s * sub, 8), sub)
        there = pl.ds(pl.multiple_of(s * sub, 8), sub)

        def send(src, sem, arrival, device):
            return pltpu.make_async_remote_copy(
                src_ref=src,
                dst_ref=in_v.at[b, here],
                send_sem=sem,
                recv_sem=arrival,
                device_id=device,
                device_id_type=MESH,
            )

        target = comp + jnp.where(low < lows - 3, 4, 2).astype(jnp.int32)
        forward = send(o_v.at[b, there], ch_send, ch_recv.at[i], (target, feat))
        back = send(in_v.at[b, here], lf_send, ch_recv.at[i], left)
        relay = send(in_v.at[b, here], rl_send, rl_recv.at[b], partner)
        return here, there, forward, back, relay

    def finish(b):
        other = pl.ds(pl.multiple_of((1 - core) * half, 8), half)
        landed(in_v.at[b, other], rl_recv.at[b])
        columns = pl.ds(pl.multiple_of(b * 128, 128), 128)
        new_v[:, columns] = new_v[:, columns] - dot(xtt_v[my_group, :], in_v[b], 1, 0) * (step_rate / rows)

    def chain(b, carry):
        @pl.when(starts)
        def _():
            add_own(b)

        def one(s, carry):
            here, there, forward, back, relay = hop(b, s)

            @pl.when(fed)
            def _():
                landed(in_v.at[b, here], ch_recv.at[b * subs + s])

                @pl.when(forwards)
                def _():
                    o_v[b, there] = in_v[b, here] + own_v[b, there]
                    forward.start()

                @pl.when(heads)
                def _():
                    back.start()

                relay.start()

            @pl.when(starts)
            def _():
                o_v[b, there] = own_v[b, there]
                forward.start()

            return carry

        lax.fori_loop(0, subs, one, 0)

        @pl.when(jnp.logical_and(jnp.logical_and(fed, jnp.logical_not(forwards)), b > 0))
        def _():
            finish(b - 1)

        return carry

    lax.fori_loop(0, blocks, chain, 0)

    @pl.when(jnp.logical_and(fed, jnp.logical_not(forwards)))
    def _():
        finish(blocks - 1)

    @pl.when(late)
    def _():
        base()

    @pl.when(jnp.logical_and(fed, forwards))
    def _():
        def finish_all(b, carry):
            finish(b)
            return carry

        lax.fori_loop(0, blocks, finish_all, 0)

    squares = jnp.zeros((group, 128), jnp.float32)
    for b in range(blocks):
        piece = new_v[:, b * 128 : (b + 1) * 128]
        squares = squares + piece * piece
    column = jnp.sum(squares, axis=1, keepdims=True)
    eye_half = lax.broadcasted_iota(jnp.int32, (group, 128), 0) == lax.broadcasted_iota(
        jnp.int32, (group, 128), 1
    )
    fin_v[feat] = jnp.sum(jnp.where(eye_half, column, 0.0), axis=0, keepdims=True)

    def tell(k, high_):
        pltpu.make_async_remote_copy(
            src_ref=fin_v.at[feat],
            dst_ref=fin_v.at[feat],
            send_sem=fin_send,
            recv_sem=fin_recv,
            device_id=(comp, plane_at(k) * highs + high_),
            device_id_type=MESH,
        ).start()

    def tell_across(k, carry):
        tell(k, 1 - high)
        return carry

    def tell_plane(k, carry):
        @pl.when(k != itself)
        def _():
            tell(k, high)

        return carry

    lax.fori_loop(0, planes, tell_across, 0)
    lax.fori_loop(0, planes, tell_plane, 0)
    for b in range(blocks):
        pltpu.make_async_copy(new_v.at[:, pl.ds(b * 128, 128)], out_hbm.at[b], ld_sem.at[0]).start()

    for n in range(slots + 1):

        @pl.when(count == n)
        def _():
            landed(sent_v.at[pl.ds(0, tiles - n)], rs_send)

    lend(side, core, 0, partner).wait_send()

    @pl.when(lends)
    def _():
        lend(side, core, 1, right).wait_send()

    @pl.when(heads)
    def _():
        lend(0, core, 1, partner).wait_send()

    @pl.when(heads)
    def _():
        pass_on(x_v.at[my_tiles]).wait_send()

    @pl.when(jnp.logical_not(heads))
    def _():
        pass_on(x_v.at[my_tiles, side]).wait_send()

    for n in range(1, slots + 1):

        @pl.when(count == n)
        def _():
            @pl.when(lends)
            def _():
                landed(sent_v.at[pl.ds(0, 3 * n)], z_send)

            @pl.when(jnp.logical_not(lends))
            def _():
                landed(sent_v.at[pl.ds(0, n)], z_send)

            landed(sent_v.at[pl.ds(0, n * (planes - 1))], ag_send)

            @pl.when(heads)
            def _():
                landed(sent_v.at[pl.ds(0, n * (planes - 1))], ag_send)

    @pl.when(forwards)
    def _():
        landed(o_v, ch_send)

    @pl.when(fed)
    def _():
        landed(o_v, rl_send)

        @pl.when(heads)
        def _():
            landed(o_v, lf_send)

    landed(fin_v.at[pl.ds(0, feats - 1)], fin_recv)
    total = fin_v[0]
    for q in range(1, feats):
        total = total + fin_v[q]
    scale_ref[...] = jnp.broadcast_to(
        lax.rsqrt(
            jnp.sum(jnp.where(eye_half, jnp.broadcast_to(total, (group, 128)), 0.0), axis=1, keepdims=True)
            / features
            + epsilon
        ),
        (group, 128),
    )

    landed(fin_v.at[pl.ds(0, feats - 1)], fin_send)
    landed(out_hbm, ld_sem.at[0])


def step(planes, highs, lows, sub, owners, samples, start_vectors):
    _, rows, width = samples.shape
    group = start_vectors.shape[0]
    feats = planes * highs
    half = rows // 2
    tiles = half // 8 + 1
    blocks = width // 128
    chunks = blocks * (half // sub)
    slots = max(owners.count(plane) for plane in owners)
    dma = pltpu.SemaphoreType.DMA
    f32 = jnp.float32
    updated, scale = pl.pallas_call(
        functools.partial(kernel, planes, highs, lows, sub, owners, width * feats),
        out_shape=(
            jax.ShapeDtypeStruct((blocks, group, 128), f32),
            jax.ShapeDtypeStruct((group, 128), f32),
        ),
        in_specs=[pl.BlockSpec(memory_space=pl.ANY)] * 2,
        out_specs=(pl.BlockSpec(memory_space=pl.ANY), pl.BlockSpec(memory_space=pltpu.VMEM)),
        scratch_shapes=[
            pltpu.VMEM((group, width), f32),
            pltpu.VMEM((rows, width), f32),
            pltpu.VMEM((3 * group, width), f32),
            pltpu.VMEM((4 * group, width), f32),
            pltpu.VMEM((tiles, 8, 128), f32),
            pltpu.VMEM((slots, planes, 8, 128), f32),
            pltpu.VMEM((slots, 8, 128), f32),
            pltpu.VMEM((2, 2, slots, 8, 128), f32),
            pltpu.VMEM((slots, 2, 8, 128), f32),
            pltpu.VMEM((2 * tiles, 2, 8, 128), f32),
            pltpu.VMEM((2, 2 * group, width), f32),
            pltpu.VMEM((2, rows, 128), f32),
            pltpu.VMEM((2, half, 128), f32),
            pltpu.VMEM((128, rows), f32),
            pltpu.VMEM((blocks, half, 128), f32),
            pltpu.VMEM((blocks, rows, 128), f32),
            pltpu.VMEM((blocks, half, 128), f32),
            pltpu.VMEM((feats, 1, 128), f32),
            pltpu.VMEM((slots * planes, 8, 128), f32),
            dma((4,)),
            dma((2,)),
            dma((2, 2)),
            dma,
            dma,
            dma,
            dma((2, 2)),
            dma,
            dma,
            dma,
            dma,
            dma,
            dma,
            dma((chunks,)),
            dma,
            dma((blocks,)),
            dma,
            dma,
            pltpu.SemaphoreType.REGULAR,
        ],
        compiler_params=pltpu.CompilerParams(collective_id=0, has_side_effects=True, vmem_limit_bytes=54900 * 1024),
    )(samples, start_vectors)
    return (updated * scale).transpose(1, 0, 2).reshape(group, width)


def solution(mesh, sub=SUB, owners=OWNERS, planes=16, highs=2, lows=8):
    in_specs = (P(None, None, "feat"), P("comp", "feat"))
    return jax.shard_map(
        functools.partial(step, planes, highs, lows, sub, owners),
        mesh=mesh,
        in_specs=in_specs,
        out_specs=P("comp", "feat"),
        check_vma=False,
    )
```
